32 devices in a mesh: groups: 2 (over x), coarse: 2 (over core), fine: 8 (over z, y).
Axes of the slice: x: 2, y: 2, z: 4, core: 2. Of those that a mesh axis runs over, the one named last changes fastest.
Arguments:
- amplitudes: float32 [32, 4], P(('groups', 'coarse', 'fine')), parts along dimension 0, may hold values from -1 to 1
- control_index: int32 [32, 4], P(('groups', 'coarse', 'fine')), parts along dimension 0, may hold values from 0 to 7
- controls: float32 [8, 512, 512], replicated, may hold values from -0.25 to 0.25
- drift_term: float32 [512, 512], replicated, may hold values from -0.25 to 0.25
- target: float32 [1024, 512], P('groups'), parts along dimension 0, may hold values from -1.5 to 1.5
Outputs:
- gradient: float32 [32, 4], P(('groups', 'coarse', 'fine')), parts along dimension 0
The draws below stay inside these ranges and needn't reach their ends.
There are 2 independent parts, one for each index of `groups`. The reference program is written for one: setup_inputs(seed, part) draws one part's arguments, and reference() takes and returns one part's arrays. A program takes and returns all parts, laid end to end along the dimension named above; an argument that names none is the same for every part. Nothing has to cross between parts.
All inputs are finite; a program needn't handle non-finite values.
Results may differ from the reference program's by a relative error of at most 0.0003.
Values sent between devices are 32-bit elements; how exact they have to be, the bound alone decides.
No kernel may reach another device: no remote copies, remote signals or barrier semaphores. Data moves between devices by JAX's collectives and lax.ppermute only.
A program may use at most 192 MiB of HBM per device.

```python
import jax
import jax.numpy as jnp
from jax import lax

M = 512
K = 8
C = 4
TAYLOR = 6
SLICES = 16


def plant(drawn, own_key, least, largest):
    index_at = [jax.random.randint(jax.random.fold_in(own_key, axis), (), 0, length) for axis, length in enumerate(drawn.shape)]
    longest = drawn.shape.index(max(drawn.shape))
    beside = index_at[:longest] + [(index_at[longest] + 1) % drawn.shape[longest]] + index_at[longest + 1:]
    return drawn.at[tuple(index_at)].set(least).at[tuple(beside)].set(largest)


def block_scale(rng, extent, pieces, smallest, largest):
    def one(dim, parts):
        steps = jax.random.uniform(jax.random.fold_in(jax.random.fold_in(rng, 6), dim), (parts,), jnp.float32, smallest / len(pieces), largest / len(pieces))
        return jnp.repeat(jnp.exp(steps), extent[dim] // parts).reshape((-1,) + (1,) * (len(extent) - dim - 1))

    level = one(*pieces[0])
    for cut in pieces[1:]:
        level = level * one(*cut)
    return level


def scatter_about(rng, extent, scale, reach, kind=jnp.bfloat16):
    return jnp.clip(scale * jax.random.normal(rng, extent, jnp.float32), -reach, reach).astype(kind)


def setup_inputs(seed: int = 0, part: int = 0) -> dict:
    splits = jax.random.split(jax.random.key(seed), 6)
    own_keys = jax.random.split(jax.random.fold_in(splits[5], part), 6)
    amplitudes = jnp.clip(jax.random.uniform(own_keys[0], (SLICES, C), jnp.float32, -1.0, 1.0) * block_scale(own_keys[0], (SLICES, C), ((0, 16),), -0.4, 0.0), -1.0, 1.0)
    control_index = plant(jax.random.randint(own_keys[1], (SLICES, C), 0, K), jax.random.fold_in(own_keys[1], 1), 0, K - 1).astype(jnp.int32)
    controls = scatter_about(splits[2], (K, M, M), M ** -0.5, 0.25, jnp.float32)
    drift_term = scatter_about(splits[3], (M, M), M ** -0.5, 0.25, jnp.float32)
    target = scatter_about(own_keys[4], (M, M), 0.25, 1.5, jnp.float32)
    return dict(amplitudes=amplitudes, control_index=control_index, controls=controls, drift_term=drift_term, target=target)


step_scale = 0.3
highest = lax.Precision.HIGHEST


def slice_weights(amplitudes, control_index):
    onehot = (control_index[:, :, None] == jnp.arange(K, dtype=jnp.int32)[None, None, :]).astype(jnp.float32)
    return onehot, jnp.sum(amplitudes[:, :, None] * onehot, axis=1)


def propagator(weights_row, controls, drift_term):
    combo = drift_term + jnp.einsum("k,kab->ab", weights_row, controls, precision=highest)
    generator = step_scale * 0.5 * (combo - combo.T)
    identity = jnp.eye(M, dtype=jnp.float32)
    series = identity + generator / TAYLOR
    for order in range(TAYLOR - 1, 0, -1):
        series = identity + jnp.dot(generator, series, precision=highest) / order
    return series


def reference(amplitudes, control_index, controls, drift_term, target):
    onehot, weights = slice_weights(amplitudes, control_index)
    identity = jnp.eye(M, dtype=jnp.float32)

    def forward(running, row):
        return jnp.dot(propagator(row, controls, drift_term), running, precision=highest), None

    total, _ = lax.scan(forward, identity, weights)
    intersection = jnp.dot(total.T, target, precision=highest)

    def second(running, inputs):
        row, hot = inputs
        running = jnp.dot(propagator(row, controls, drift_term), running, precision=highest)
        aligned = jnp.dot(jnp.dot(running, intersection, precision=highest), running.T, precision=highest)
        skew = 0.5 * (aligned - aligned.T)
        inner = jnp.einsum("kab,ab->k", controls, skew, precision=highest)
        return running, step_scale * jnp.dot(hot, inner, precision=highest)

    _, gradient = lax.scan(second, identity, (weights, onehot))
    return gradient
```

```python
import functools

import jax
import jax.numpy as jnp
from jax import lax
from jax.experimental import pallas as pl
from jax.experimental.pallas import tpu as pltpu
from jax.sharding import PartitionSpec as P

step_scale = 0.3
f32 = jnp.float32
bf16 = jnp.bfloat16


def split(x):
    high = x.astype(bf16)
    return high, (x - high.astype(f32)).astype(bf16)


def dot(a, b):
    return jnp.dot(a, b, preferred_element_type=f32)


def dot_nt(a, b):
    return lax.dot_general(a, b, (((1,), (1,)), ((), ())), preferred_element_type=f32)


def col_blocks(m):
    width = 256 if m % 256 == 0 else m
    return [slice(at, at + width) for at in range(0, m, width)]


def row_blocks(m, height):
    height = height if m % height == 0 else m
    return [slice(at, at + height) for at in range(0, m, height)]


def tiles(m):
    width = 128 if m % 128 == 0 else m
    return [slice(at, at + width) for at in range(0, m, width)]


def dot3(ah, al, bh, bl, cols):
    return dot(ah[...], bh[:, cols]) + dot(ah[...], bl[:, cols]) + dot(al[...], bh[:, cols])


def block_kernel(
    count, order, place, rows, controls, drift, target, send, local,
    mix, ah, al, a32, bh, bl, b32, dh, dl, d32, qh, ql, wh, wl, run, rh, rl,
):
    m = drift.shape[0]
    half = step_scale * 0.5
    coarse = place[0]
    fine = place[1]

    def generator(step):
        row = step ^ fine
        amps = [rows[row, c] for c in range(count)]
        picks = [rows[row, count + c].astype(jnp.int32) for c in range(count)]
        for rs in row_blocks(m, 32):
            total = drift[rs, :]
            for c in range(count):
                total = total + amps[c] * controls[picks[c], rs, :]
            mix[rs, :] = total
        for i, ti in enumerate(tiles(m)):
            for j, tj in enumerate(tiles(m)):
                if j > i:
                    continue
                value = half * (mix[ti, tj] - mix[tj, ti].T)
                high, low = split(value)
                a32[ti, tj] = value
                ah[ti, tj] = high
                al[ti, tj] = low
                if j < i:
                    back = -value.T
                    high, low = split(back)
                    a32[tj, ti] = back
                    ah[tj, ti] = high
                    al[tj, ti] = low

    def propagator():
        for cs in col_blocks(m):
            value = dot3(ah, al, ah, al, cs)
            b32[:, cs] = value
            bh[:, cs], bl[:, cs] = split(value)
        for cs in col_blocks(m):
            value = dot3(ah, al, bh, bl, cs)
            d32[:, cs] = value
            dh[:, cs], dl[:, cs] = split(value)
            rest = a32[:, cs] * (1 / 24) + b32[:, cs] * (1 / 120) + value * (1 / 720)
            qh[:, cs], ql[:, cs] = split(rest)
        for cs in col_blocks(m):
            value = dot3(dh, dl, qh, ql, cs)
            value = value + a32[:, cs] + b32[:, cs] * 0.5 + d32[:, cs] * (1 / 6)
            d32[:, cs] = value
            wh[:, cs], wl[:, cs] = split(value)

    def keep(step):
        @pl.when(step == fine)
        def _():
            for rs in row_blocks(m, 32):
                local[rs, :] = run[rs, :]

    generator(0)
    propagator()
    for rs in row_blocks(m, 32):
        at = lax.broadcasted_iota(jnp.int32, (rs.stop - rs.start, m), 0) + rs.start
        eye = (at == lax.broadcasted_iota(jnp.int32, (rs.stop - rs.start, m), 1)).astype(f32)
        value = d32[rs, :] + eye
        run[rs, :] = value
        rh[rs, :], rl[rs, :] = split(value)
    keep(0)

    def body(step, carry):
        generator(step)
        propagator()
        for cs in col_blocks(m):
            value = dot3(wh, wl, rh, rl, cs) + run[:, cs]
            run[:, cs] = value
            rh[:, cs], rl[:, cs] = split(value)
        keep(step)
        return carry

    lax.fori_loop(1, order, body, 0)

    @pl.when(coarse == 0)
    def _():
        for rs in row_blocks(m, 32):
            send[rs, :] = run[rs, :]

    @pl.when(coarse != 0)
    def _():
        for ti in tiles(m):
            for tj in tiles(m):
                qh[ti, tj], ql[ti, tj] = split(target[tj, ti].T)
        for cs in col_blocks(m):
            send[:, cs] = dot3(qh, ql, rh, rl, cs)


def final_kernel(
    count, place, picks, sent, got, local, controls, out,
    ph, plo, bh, bl, vh, vl, x32, kh, kl, uh, ul, g32,
):
    m = local.shape[0]
    coarse = place[0]

    def load(first, second):
        for rs in row_blocks(m, 32):
            bh[rs, :], bl[rs, :] = split(first[rs, :])
            vh[rs, :], vl[rs, :] = split(second[rs, :])
            ph[rs, :], plo[rs, :] = split(local[rs, :])

    @pl.when(coarse == 0)
    def _():
        load(sent, got)

    @pl.when(coarse != 0)
    def _():
        load(got, sent)
        for cs in col_blocks(m):
            uh[:, cs], ul[:, cs] = split(dot3(ph, plo, bh, bl, cs))
        for rs in row_blocks(m, 64):
            ph[rs, :] = uh[rs, :]
            plo[rs, :] = ul[rs, :]

    for cs in col_blocks(m):
        x32[:, cs] = dot3(vh, vl, bh, bl, cs)
    for ti in tiles(m):
        for tj in tiles(m):
            kh[ti, tj], kl[ti, tj] = split(0.5 * (x32[tj, ti].T - x32[ti, tj]))
    for cs in col_blocks(m):
        uh[:, cs], ul[:, cs] = split(dot3(ph, plo, kh, kl, cs))
    for cs in col_blocks(m):
        g32[:, cs] = (
            dot_nt(uh[...], ph[cs, :]) + dot_nt(uh[...], plo[cs, :]) + dot_nt(ul[...], ph[cs, :])
        )
    for c in range(count):
        pick = picks[0, c]
        total = jnp.zeros((8, m), f32)
        for rs in row_blocks(m, 8):
            total = total + controls[pick, rs, :] * g32[rs, :]
        out[0, c] = step_scale * jnp.sum(total)


def on_device(amplitudes, control_index, controls, drift_term, target):
    m = target.shape[0]
    count = amplitudes.shape[1]
    order = lax.axis_size("fine")
    assert amplitudes.shape[0] == 1 and lax.axis_size("coarse") == 2 and order & (order - 1) == 0
    place = jnp.stack([lax.axis_index("coarse"), lax.axis_index("fine")]).astype(jnp.int32)
    rows = jnp.concatenate([amplitudes, control_index.astype(f32)], axis=1)
    bit = 1
    while bit < order:
        swap = [(i, i ^ bit) for i in range(order)]
        rows = jnp.concatenate([rows, lax.ppermute(rows, "fine", swap)], axis=0)
        bit *= 2

    smem = pl.BlockSpec(memory_space=pltpu.SMEM)
    vmem = pl.BlockSpec(memory_space=pltpu.VMEM)
    full, half = pltpu.VMEM((m, m), f32), pltpu.VMEM((m, m), bf16)
    square = jax.ShapeDtypeStruct((m, m), f32)
    send, local = pl.pallas_call(
        functools.partial(block_kernel, count, order),
        out_shape=(square, square),
        in_specs=[smem, smem, vmem, vmem, vmem],
        out_specs=(vmem, vmem),
        scratch_shapes=[
            full, half, half, full, half, half, full, half, half, full,
            half, half, half, half, full, half, half,
        ],
        compiler_params=pltpu.CompilerParams(vmem_limit_bytes=48 << 20),
        name="block",
    )(place, rows, controls, drift_term, target)
    got = lax.ppermute(send, "coarse", [(0, 1), (1, 0)])
    return pl.pallas_call(
        functools.partial(final_kernel, count),
        out_shape=jax.ShapeDtypeStruct((1, count), f32),
        in_specs=[smem, smem, vmem, vmem, vmem, vmem],
        out_specs=smem,
        scratch_shapes=[half, half, half, half, half, half, full, half, half, half, half, full],
        compiler_params=pltpu.CompilerParams(vmem_limit_bytes=48 << 20),
        name="final",
    )(place, control_index, send, got, local, controls)


def solution(mesh):
    placed = (
        P(("groups", "coarse", "fine"), None),
        P(("groups", "coarse", "fine"), None),
        P(),
        P(),
        P("groups", None),
    )
    return jax.shard_map(
        on_device,
        mesh=mesh,
        in_specs=placed,
        out_specs=P(("groups", "coarse", "fine"), None),
        check_vma=False,
    )
```

```python
import functools

import jax
import jax.numpy as jnp
from jax import lax
from jax.experimental import pallas as pl
from jax.experimental.pallas import tpu as pltpu
from jax.sharding import PartitionSpec as P

step_scale = 0.3
f32 = jnp.float32
bf16 = jnp.bfloat16
SMEM = pl.BlockSpec(memory_space=pltpu.SMEM)
VMEM = pl.BlockSpec(memory_space=pltpu.VMEM)
HBM = pl.BlockSpec(memory_space=pltpu.HBM)


def split(x):
    high = x.astype(bf16)
    return high, (x - high.astype(f32)).astype(bf16)


def dot(a, b):
    return jnp.dot(a, b, preferred_element_type=f32)


def dot_nt(a, b):
    return lax.dot_general(a, b, (((1,), (1,)), ((), ())), preferred_element_type=f32)


def pieces(m, size):
    size = size if m % size == 0 else m
    return [slice(at, at + size) for at in range(0, m, size)]


def dot3(ah, al, bh, bl, cols, rows=slice(None)):
    return (
        dot(ah[rows, :], bh[:, cols])
        + dot(ah[rows, :], bl[:, cols])
        + dot(al[rows, :], bh[:, cols])
    )


def generator(amps, picks, table, drift, s):
    m = drift.shape[0]
    half = step_scale * 0.5
    for rs in pieces(m, 32):
        total = drift[rs, :]
        for amp, pick in zip(amps, picks):
            total = total + amp * table[pick, rs, :]
        s.mix[rs, :] = total
    for i, ti in enumerate(pieces(m, 128)):
        for tj in pieces(m, 128)[: i + 1]:
            value = half * (s.mix[ti, tj] - s.mix[tj, ti].T)
            s.a32[ti, tj] = value
            s.ah[ti, tj], s.al[ti, tj] = split(value)
            if ti != tj:
                back = -value.T
                s.a32[tj, ti] = back
                s.ah[tj, ti], s.al[tj, ti] = split(back)


def mirrored(ah, al, bh, bl, sign, put):
    m = ah.shape[0]
    for cs in pieces(m, 256):
        value = dot3(ah, al, bh, bl, cs, slice(cs.start, m))
        put(slice(cs.start, m), cs, value)
        width = cs.stop - cs.start
        for rs in pieces(m, 256):
            if rs.start > cs.start:
                at = rs.start - cs.start
                flipped = value[at : at + width, :].T
                put(cs, rs, flipped if sign > 0 else -flipped)


def square_step(s):
    def put(rows, cols, value):
        s.b32[rows, cols] = value
        s.bh[rows, cols], s.bl[rows, cols] = split(value)

    mirrored(s.ah, s.al, s.ah, s.al, 1, put)


def cube_step(s):
    def put(rows, cols, value):
        s.dh[rows, cols], s.dl[rows, cols] = split(value)
        a, b = s.a32[rows, cols], s.b32[rows, cols]
        rest = a * (1 / 24) + b * (1 / 120) + value * (1 / 720)
        s.qh[rows, cols], s.ql[rows, cols] = split(rest)
        s.a32[rows, cols] = a + b * 0.5 + value * (1 / 6)

    mirrored(s.ah, s.al, s.bh, s.bl, -1, put)


def last_step(s, wh, wl):
    for cs in pieces(s.ah.shape[0], 256):
        value = dot3(s.dh, s.dl, s.qh, s.ql, cs) + s.a32[:, cs]
        wh[:, cs], wl[:, cs] = split(value)


def inside(x):
    return pltpu.with_memory_space_constraint(x, pltpu.VMEM)


def outside(x):
    return pltpu.with_memory_space_constraint(x, pltpu.HBM)


class Work:
    names = ("mix", "a32", "b32", "ah", "al", "bh", "bl", "dh", "dl", "qh", "ql")

    def __init__(self, refs):
        for name, ref in zip(self.names, refs):
            setattr(self, name, ref)

    @classmethod
    def shapes(cls, m):
        return [pltpu.VMEM((m, m), f32)] * 3 + [pltpu.VMEM((m, m), bf16)] * 8


def propagators(rows, picked, table, works, wh, wl, first):
    count = rows.shape[1] // 2
    drift = table.at[table.shape[0] - 1]
    for row, s in zip(picked, works):
        amps = [rows[row, c] for c in range(count)]
        picks = [rows[row, count + c].astype(jnp.int32) for c in range(count)]
        generator(amps, picks, table, drift, s)
    for s in works:
        square_step(s)
    for s in works:
        cube_step(s)
    for k, (row, s) in enumerate(zip(picked, works)):
        slot = k if first is None else first + row
        last_step(s, wh.at[slot], wl.at[slot])


def first_kernel(amps, picks, controls, drift, table, wh, wl, mine, *scratch):
    sems = scratch[-1]
    kinds, count = controls.shape[0], amps.shape[1]
    own = [pltpu.make_async_copy(drift, mine.at[count], sems.at[count])]
    for c in range(count):
        own.append(pltpu.make_async_copy(controls.at[picks[0, c]], mine.at[c], sems.at[c]))
    rest = [pltpu.make_async_copy(drift, table.at[kinds], sems.at[count + 1 + kinds])]
    for k in range(kinds):
        rest.append(pltpu.make_async_copy(controls.at[k], table.at[k], sems.at[count + 1 + k]))
    for copy in own + rest:
        copy.start()
    for copy in own:
        copy.wait()
    s = Work(scratch[:-1])
    generator([amps[0, c] for c in range(count)], list(range(count)), mine, mine.at[count], s)
    square_step(s)
    cube_step(s)
    last_step(s, wh.at[0], wl.at[0])
    for copy in rest:
        copy.wait()


def build_kernel(first, rows, table, wh_in, wl_in, wh, wl, *scratch):
    size = len(Work.names)
    slots = rows.shape[0]
    works = [Work(scratch[n * size : (n + 1) * size]) for n in range(len(scratch) // size)]
    for n in range(0, slots, len(works)):
        propagators(rows, range(n, n + len(works)), table, works, wh, wl, first)


def chain_kernel(order, place, rows, table, wh_in, wl_in, run, local, wh, wl, rh, rl, both, *scratch):
    size = len(Work.names)
    works = [Work(scratch[n * size : (n + 1) * size]) for n in range(2)]
    m = run.shape[0]
    fine = place[1]
    first = order - rows.shape[0]

    def pair(n, carry):
        propagators(rows, [2 * n, 2 * n + 1], table, works, wh, wl, first)
        return carry

    lax.fori_loop(0, rows.shape[0] // 2, pair, 0)
    start_product(fine, wh.at[fine], wl.at[fine], run, rh, rl)
    for rs in pieces(m, 32):
        both[0, rs, :] = run[rs, :]
    for step in range(1, order):
        slot = step ^ fine
        side = jnp.where(step <= fine, 0, 1)
        for cs in pieces(m, 256):
            value = dot3(wh.at[slot], wl.at[slot], rh, rl, cs) + run[:, cs]
            run[:, cs] = value
            both[side, :, cs] = value
            rh[:, cs], rl[:, cs] = split(value)
    for rs in pieces(m, 32):
        local[rs, :] = both[0, rs, :]


def long_kernel(order, place, rows, table, run, local, wh, wl, rh, rl, *scratch):
    size = len(Work.names)
    works = [Work(scratch[n * size : (n + 1) * size]) for n in range(2)]
    m = run.shape[0]
    fine = place[1]
    for rs in pieces(m, 32):
        value = unit(rs, m)
        run[rs, :] = value
        rh[rs, :], rl[rs, :] = split(value)

    def pair(n, carry):
        steps = [2 * n, 2 * n + 1]
        propagators(rows, [step ^ fine for step in steps], table, works, wh, wl, None)
        for k, step in enumerate(steps):
            for cs in pieces(m, 256):
                value = dot3(wh.at[k], wl.at[k], rh, rl, cs) + run[:, cs]
                run[:, cs] = value
                rh[:, cs], rl[:, cs] = split(value)

            @pl.when(step == fine)
            def _():
                for rs in pieces(m, 32):
                    local[rs, :] = run[rs, :]

        return carry

    lax.fori_loop(0, order // 2, pair, 0)


def unit(rs, m):
    at = lax.broadcasted_iota(jnp.int32, (rs.stop - rs.start, m), 0) + rs.start
    return (at == lax.broadcasted_iota(jnp.int32, (rs.stop - rs.start, m), 1)).astype(f32)


def start_product(fine, wh, wl, run, rh, rl):
    m = run.shape[0]
    for rs in pieces(m, 32):
        value = wh[rs, :].astype(f32) + wl[rs, :].astype(f32) + unit(rs, m)
        run[rs, :] = value
        rh[rs, :], rl[rs, :] = split(value)


def target_kernel(run, target, out, th, tl, bh, bl):
    m = target.shape[0]
    for ti in pieces(m, 128):
        bh[ti, :], bl[ti, :] = split(run[ti, :])
        for tj in pieces(m, 128):
            th[ti, tj], tl[ti, tj] = split(target[tj, ti].T)
    for cs in pieces(m, 256):
        out[:, cs] = dot3(th, tl, bh, bl, cs)


def final_kernel(
    count, place, picks, run, got, turned, th, tl, local, table, out,
    ph, plo, bh, bl, vh, vl, x32, kh, kl, uh, ul, g32,
):
    m = local.shape[0]
    coarse = place[0]

    @pl.when(coarse == 0)
    def _():
        for rs in pieces(m, 32):
            uh[rs, :], ul[rs, :] = split(got[rs, :])
            bh[rs, :], bl[rs, :] = split(run[rs, :])
            ph[rs, :], plo[rs, :] = split(local[rs, :])
        for cs in pieces(m, 256):
            vh[:, cs], vl[:, cs] = split(dot3(th, tl, uh, ul, cs))
        for cs in pieces(m, 256):
            x32[:, cs] = dot3(vh, vl, bh, bl, cs)

    @pl.when(coarse != 0)
    def _():
        for rs in pieces(m, 32):
            bh[rs, :], bl[rs, :] = split(got[rs, :])
            vh[rs, :], vl[rs, :] = split(turned[rs, :])
            uh[rs, :], ul[rs, :] = split(local[rs, :])
        for cs in pieces(m, 256):
            x32[:, cs] = dot3(vh, vl, bh, bl, cs)
        for cs in pieces(m, 256):
            ph[:, cs], plo[:, cs] = split(dot3(uh, ul, bh, bl, cs))

    for i, ti in enumerate(pieces(m, 128)):
        for tj in pieces(m, 128)[: i + 1]:
            value = 0.5 * (x32[tj, ti].T - x32[ti, tj])
            kh[ti, tj], kl[ti, tj] = split(value)
            if ti != tj:
                kh[tj, ti], kl[tj, ti] = split(-value.T)
    for cs in pieces(m, 256):
        uh[:, cs], ul[:, cs] = split(dot3(ph, plo, kh, kl, cs))
    for cs in pieces(m, 256):
        g32[:, cs] = (
            dot_nt(uh[...], ph[cs, :]) + dot_nt(uh[...], plo[cs, :]) + dot_nt(ul[...], ph[cs, :])
        )
    for c in range(count):
        total = jnp.zeros((8, m), f32)
        for rs in pieces(m, 8):
            total = total + table[picks[0, c], rs, :] * g32[rs, :]
        out[0, c] = step_scale * jnp.sum(total)


def on_device(amplitudes, control_index, controls, drift_term, target):
    m = target.shape[0]
    kinds, count = controls.shape[0], amplitudes.shape[1]
    order = lax.axis_size("fine")
    assert amplitudes.shape[0] == 1 and lax.axis_size("coarse") == 2
    assert order & (order - 1) == 0 and order >= 4
    place = jnp.stack([lax.axis_index("coarse"), lax.axis_index("fine")]).astype(jnp.int32)
    square, half = pltpu.VMEM((m, m), f32), pltpu.VMEM((m, m), bf16)
    full = pltpu.VMEM((m, m), f32)
    short = order <= 8

    def params(mib):
        return pltpu.CompilerParams(vmem_limit_bytes=mib << 20)

    def cost(products):
        return pl.CostEstimate(
            flops=6 * products * m**3, bytes_accessed=12 * products * m * m, transcendentals=0
        )

    rows = jnp.concatenate([amplitudes, control_index.astype(f32)], axis=1)
    table = wh = wl = other = None
    bit = 1
    while bit < order:
        swap = [(i, i ^ bit) for i in range(order)]
        coming = lax.ppermute(rows, "fine", swap)
        if bit == 1:
            slots = 8 if short else 1
            slots = min(slots, order)
            halves = pltpu.VMEM((slots, m, m), bf16)
            table, wh, wl = pl.pallas_call(
                first_kernel,
                out_shape=(pltpu.VMEM((kinds + 1, m, m), f32), halves, halves),
                in_specs=[SMEM, SMEM, HBM, HBM],
                out_specs=(VMEM, VMEM, VMEM),
                scratch_shapes=[
                    pltpu.VMEM((count + 1, m, m), f32), *Work.shapes(m),
                    pltpu.SemaphoreType.DMA((count + kinds + 2,)),
                ],
                compiler_params=params(FIRST_MIB),
                cost_estimate=cost(4),
                name="first",
            )(amplitudes, control_index, outside(controls), outside(drift_term))
        elif short:
            width = min(2, bit // 2)
            wh, wl = pl.pallas_call(
                functools.partial(build_kernel, bit // 2),
                out_shape=(halves, halves),
                in_specs=[SMEM, VMEM, VMEM, VMEM],
                out_specs=(VMEM, VMEM),
                scratch_shapes=Work.shapes(m) * width,
                input_output_aliases={2: 0, 3: 1},
                compiler_params=params(BUILD_MIB),
                cost_estimate=cost(4 * bit // 2),
                name="build",
            )(other, *map(inside, (table, wh, wl)))
        other = coming
        rows = jnp.concatenate([rows, other], axis=0)
        bit *= 2

    if short:
        kernel, taken, first = chain_kernel, (other, table, wh, wl), order - other.shape[0]
        outs, aliases = (square, square, halves, halves), {3: 2, 4: 3}
        scratch = [half, half, pltpu.VMEM((2, m, m), f32)]
    else:
        kernel, taken = long_kernel, (rows, table)
        outs, aliases = (square, square), {}
        scratch = [pltpu.VMEM((2, m, m), bf16), pltpu.VMEM((2, m, m), bf16), half, half]
    run, local = pl.pallas_call(
        functools.partial(kernel, order),
        out_shape=outs,
        in_specs=[SMEM, SMEM] + [VMEM] * (len(taken) - 1),
        out_specs=(VMEM,) * len(outs),
        scratch_shapes=[*scratch, *Work.shapes(m) * 2],
        input_output_aliases=aliases,
        compiler_params=params(CHAIN_MIB),
        cost_estimate=cost(23),
        name="chain",
    )(place, taken[0], *map(inside, taken[1:]))[:2]
    got = lax.ppermute(run, "coarse", [(0, 1), (1, 0)])
    turned, th, tl = pl.pallas_call(
        target_kernel,
        out_shape=(square, half, half),
        in_specs=[VMEM, VMEM],
        out_specs=(VMEM, VMEM, VMEM),
        scratch_shapes=[half] * 2,
        compiler_params=params(TURN_MIB),
        cost_estimate=cost(1),
        name="turn",
    )(run, target)
    return pl.pallas_call(
        functools.partial(final_kernel, count),
        out_shape=jax.ShapeDtypeStruct((1, count), f32),
        in_specs=[SMEM, SMEM] + [VMEM] * 7,
        out_specs=SMEM,
        scratch_shapes=[half, half, half, half, half, half, full, half, half, half, half, full],
        compiler_params=params(FINAL_MIB),
        name="final",
    )(place, control_index, run, got, *map(inside, (turned, th, tl, local, table)))


FIRST_MIB = 16
BUILD_MIB = 16
CHAIN_MIB = 20
TURN_MIB = 6
FINAL_MIB = 12


def solution(mesh):
    placed = (
        P(("groups", "coarse", "fine"), None),
        P(("groups", "coarse", "fine"), None),
        P(),
        P(),
        P("groups", None),
    )
    return jax.shard_map(
        on_device,
        mesh=mesh,
        in_specs=placed,
        out_specs=P(("groups", "coarse", "fine"), None),
        check_vma=False,
    )
```

```python
import functools

import jax
import jax.numpy as jnp
from jax import lax
from jax.experimental import pallas as pl
from jax.experimental.pallas import tpu as pltpu
from jax.sharding import PartitionSpec as P

step_scale = 0.3
f32 = jnp.float32
bf16 = jnp.bfloat16
SMEM = pl.BlockSpec(memory_space=pltpu.SMEM)
VMEM = pl.BlockSpec(memory_space=pltpu.VMEM)
HBM = pl.BlockSpec(memory_space=pltpu.HBM)


def split(x):
    high = x.astype(bf16)
    return high, (x - high.astype(f32)).astype(bf16)


def dot(a, b):
    return jnp.dot(a, b, preferred_element_type=f32)


def dot_nt(a, b):
    return lax.dot_general(a, b, (((1,), (1,)), ((), ())), preferred_element_type=f32)


def pieces(m, size):
    size = size if m % size == 0 else m
    return [slice(at, at + size) for at in range(0, m, size)]


def dot3(ah, al, bh, bl, cols, rows=slice(None)):
    return (
        dot(ah[rows, :], bh[:, cols])
        + dot(ah[rows, :], bl[:, cols])
        + dot(al[rows, :], bh[:, cols])
    )


def generator(amps, picks, table, drift, s):
    m = drift.shape[0]
    half = step_scale * 0.5
    for rs in pieces(m, 32):
        total = drift[rs, :]
        for amp, pick in zip(amps, picks):
            total = total + amp * table[pick, rs, :]
        s.mix[rs, :] = total
    for i, ti in enumerate(pieces(m, 128)):
        for tj in pieces(m, 128)[: i + 1]:
            value = half * (s.mix[ti, tj] - s.mix[tj, ti].T)
            s.a32[ti, tj] = value
            s.ah[ti, tj], s.al[ti, tj] = split(value)
            if ti != tj:
                back = -value.T
                s.a32[tj, ti] = back
                s.ah[tj, ti], s.al[tj, ti] = split(back)


def mirrored(ah, al, bh, bl, sign, put):
    m = ah.shape[0]
    for cs in pieces(m, 256):
        value = dot3(ah, al, bh, bl, cs, slice(cs.start, m))
        put(slice(cs.start, m), cs, value)
        width = cs.stop - cs.start
        for rs in pieces(m, 256):
            if rs.start > cs.start:
                at = rs.start - cs.start
                flipped = value[at : at + width, :].T
                put(cs, rs, flipped if sign > 0 else -flipped)


def square_step(s):
    def put(rows, cols, value):
        s.b32[rows, cols] = value
        s.bh[rows, cols], s.bl[rows, cols] = split(value)

    mirrored(s.ah, s.al, s.ah, s.al, 1, put)


def cube_step(s):
    def put(rows, cols, value):
        s.dh[rows, cols], s.dl[rows, cols] = split(value)
        a, b = s.a32[rows, cols], s.b32[rows, cols]
        rest = a * (1 / 24) + b * (1 / 120) + value * (1 / 720)
        s.qh[rows, cols], s.ql[rows, cols] = split(rest)
        s.a32[rows, cols] = a + b * 0.5 + value * (1 / 6)

    mirrored(s.ah, s.al, s.bh, s.bl, -1, put)


def last_step(s, wh, wl):
    for cs in pieces(s.ah.shape[0], 256):
        value = dot3(s.dh, s.dl, s.qh, s.ql, cs) + s.a32[:, cs]
        wh[:, cs], wl[:, cs] = split(value)


def inside(x):
    return pltpu.with_memory_space_constraint(x, pltpu.VMEM)


def outside(x):
    return pltpu.with_memory_space_constraint(x, pltpu.HBM)


class Work:
    names = ("mix", "a32", "b32", "ah", "al", "bh", "bl", "dh", "dl", "qh", "ql")

    def __init__(self, refs):
        for name, ref in zip(self.names, refs):
            setattr(self, name, ref)

    @classmethod
    def shapes(cls, m):
        return [pltpu.VMEM((m, m), f32)] * 3 + [pltpu.VMEM((m, m), bf16)] * 8


def propagators(rows, picked, table, works, wh, wl, first):
    count = rows.shape[1] // 2
    drift = table.at[table.shape[0] - 1]
    for row, s in zip(picked, works):
        amps = [rows[row, c] for c in range(count)]
        picks = [rows[row, count + c].astype(jnp.int32) for c in range(count)]
        generator(amps, picks, table, drift, s)
    for s in works:
        square_step(s)
    for s in works:
        cube_step(s)
    for k, (row, s) in enumerate(zip(picked, works)):
        slot = k if first is None else first + row
        last_step(s, wh.at[slot], wl.at[slot])


def first_kernel(rows, controls, drift, table, wh, wl, mine, *scratch):
    sems = scratch[-1]
    kinds, count = controls.shape[0], rows.shape[1] // 2
    own = [pltpu.make_async_copy(drift, mine.at[count], sems.at[count])]
    for c in range(count):
        pick = rows[0, count + c].astype(jnp.int32)
        own.append(pltpu.make_async_copy(controls.at[pick], mine.at[c], sems.at[c]))
    rest = [pltpu.make_async_copy(drift, table.at[kinds], sems.at[count + 1 + kinds])]
    for k in range(kinds):
        rest.append(pltpu.make_async_copy(controls.at[k], table.at[k], sems.at[count + 1 + k]))
    for copy in own:
        copy.start()
    for copy in own:
        copy.wait()
    for copy in rest:
        copy.start()
    s = Work(scratch[:-1])
    generator([rows[0, c] for c in range(count)], list(range(count)), mine, mine.at[count], s)
    square_step(s)
    cube_step(s)
    last_step(s, wh, wl)
    for copy in rest:
        copy.wait()


def multiply_on(wh, wl, run, rh, rl):
    for cs in pieces(run.shape[0], 256):
        value = dot3(wh, wl, rh, rl, cs) + run[:, cs]
        run[:, cs] = value
        rh[:, cs], rl[:, cs] = split(value)


def copy_rows(source, goal):
    for rs in pieces(goal.shape[0], 32):
        goal[rs, :] = source[rs, :]


def chain_kernel(order, place, rows, table, own_h, own_l, run, local, rh, rl, *scratch):
    fine = place[1]
    drift = table.at[table.shape[0] - 1]
    count = rows.shape[1] // 2
    others = order - 1
    mix, dh, dl, qh, ql = scratch[:5]
    works, w_refs = [], []
    for n in range(2):
        a32, ah, al, b32, bh, bl, wh, wl = scratch[5 + 8 * n : 13 + 8 * n]
        works.append(Work((mix, a32, b32, ah, al, bh, bl, dh, dl, qh, ql)))
        w_refs.append((wh, wl))

    def start(n, s):
        step = jnp.where(n < fine, n, n + 1)
        row = step ^ fine
        amps = [rows[row, c] for c in range(count)]
        picks = [rows[row, count + c].astype(jnp.int32) for c in range(count)]
        generator(amps, picks, table, drift, s)
        square_step(s)

    def stage(n, side, more):
        cube_step(works[side])
        last_step(works[side], *w_refs[side])
        if more:
            start(n + 1, works[1 - side])

    def own():
        multiply_on(own_h, own_l, run, rh, rl)
        copy_rows(run, local)

    def advance(n, side):
        @pl.when(fine == n)
        def _():
            own()

        multiply_on(*w_refs[side], run, rh, rl)

    start(0, works[0])
    stage(0, 0, True)

    @pl.when(fine == 0)
    def _():
        start_product(own_h, own_l, run, rh, rl)
        copy_rows(run, local)

    @pl.when(fine != 0)
    def _():
        for rs in pieces(run.shape[0], 32):
            value = unit(rs, run.shape[0])
            run[rs, :] = value
            rh[rs, :], rl[rs, :] = split(value)

    multiply_on(*w_refs[0], run, rh, rl)
    stage(1, 1, others > 2)

    def two(k, carry):
        n = 2 * k + 2
        advance(n - 1, 1)
        stage(n, 0, True)
        advance(n, 0)
        stage(n + 1, 1, True)
        return carry

    loops = max(others - 3, 0) // 2
    lax.fori_loop(0, loops, two, 0)
    for n in range(2 * loops + 2, others):
        advance(n - 1, (n - 1) % 2)
        stage(n, n % 2, n + 1 < others)
    advance(others - 1, (others - 1) % 2)

    @pl.when(fine == others)
    def _():
        own()


def long_kernel(order, place, rows, table, run, local, wh, wl, rh, rl, *scratch):
    size = len(Work.names)
    works = [Work(scratch[n * size : (n + 1) * size]) for n in range(2)]
    m = run.shape[0]
    fine = place[1]
    for rs in pieces(m, 32):
        value = unit(rs, m)
        run[rs, :] = value
        rh[rs, :], rl[rs, :] = split(value)

    def pair(n, carry):
        steps = [2 * n, 2 * n + 1]
        propagators(rows, [step ^ fine for step in steps], table, works, wh, wl, None)
        for k, step in enumerate(steps):
            for cs in pieces(m, 256):
                value = dot3(wh.at[k], wl.at[k], rh, rl, cs) + run[:, cs]
                run[:, cs] = value
                rh[:, cs], rl[:, cs] = split(value)

            @pl.when(step == fine)
            def _():
                for rs in pieces(m, 32):
                    local[rs, :] = run[rs, :]

        return carry

    lax.fori_loop(0, order // 2, pair, 0)


def unit(rs, m):
    at = lax.broadcasted_iota(jnp.int32, (rs.stop - rs.start, m), 0) + rs.start
    return (at == lax.broadcasted_iota(jnp.int32, (rs.stop - rs.start, m), 1)).astype(f32)


def start_product(wh, wl, run, rh, rl):
    m = run.shape[0]
    for rs in pieces(m, 32):
        value = wh[rs, :].astype(f32) + wl[rs, :].astype(f32) + unit(rs, m)
        run[rs, :] = value
        rh[rs, :], rl[rs, :] = split(value)


def flip_kernel(rows, target, table, th, tl, table_out):
    m = target.shape[0]
    for ti in pieces(m, 128):
        for tj in pieces(m, 128):
            th[ti, tj], tl[ti, tj] = split(target[tj, ti].T)


def target_kernel(run, th, tl, out, bh, bl):
    m = run.shape[0]
    for rs in pieces(m, 32):
        bh[rs, :], bl[rs, :] = split(run[rs, :])
    for cs in pieces(m, 256):
        out[:, cs] = dot3(th, tl, bh, bl, cs)


def final_kernel(
    count, place, picks, run, got, turned, th, tl, local, table, out,
    ph, plo, bh, bl, vh, vl, x32, kh, kl, uh, ul, g32,
):
    m = local.shape[0]
    coarse = place[0]

    @pl.when(coarse == 0)
    def _():
        for rs in pieces(m, 32):
            uh[rs, :], ul[rs, :] = split(got[rs, :])
            bh[rs, :], bl[rs, :] = split(run[rs, :])
            ph[rs, :], plo[rs, :] = split(local[rs, :])
        for cs in pieces(m, 256):
            vh[:, cs], vl[:, cs] = split(dot3(th, tl, uh, ul, cs))
        for cs in pieces(m, 256):
            x32[:, cs] = dot3(vh, vl, bh, bl, cs)

    @pl.when(coarse != 0)
    def _():
        for rs in pieces(m, 32):
            bh[rs, :], bl[rs, :] = split(got[rs, :])
            vh[rs, :], vl[rs, :] = split(turned[rs, :])
            uh[rs, :], ul[rs, :] = split(local[rs, :])
        for cs in pieces(m, 256):
            x32[:, cs] = dot3(vh, vl, bh, bl, cs)
        for cs in pieces(m, 256):
            ph[:, cs], plo[:, cs] = split(dot3(uh, ul, bh, bl, cs))

    for i, ti in enumerate(pieces(m, 128)):
        for tj in pieces(m, 128)[: i + 1]:
            value = 0.5 * (x32[tj, ti].T - x32[ti, tj])
            kh[ti, tj], kl[ti, tj] = split(value)
            if ti != tj:
                kh[tj, ti], kl[tj, ti] = split(-value.T)
    for cs in pieces(m, 256):
        uh[:, cs], ul[:, cs] = split(dot3(ph, plo, kh, kl, cs))
    for cs in pieces(m, 256):
        g32[:, cs] = (
            dot_nt(uh[...], ph[cs, :]) + dot_nt(uh[...], plo[cs, :]) + dot_nt(ul[...], ph[cs, :])
        )
    for c in range(count):
        total = jnp.zeros((8, m), f32)
        for rs in pieces(m, 8):
            total = total + table[picks[0, c], rs, :] * g32[rs, :]
        out[0, c] = step_scale * jnp.sum(total)


def on_device(amplitudes, control_index, controls, drift_term, target):
    m = target.shape[0]
    kinds, count = controls.shape[0], amplitudes.shape[1]
    order = lax.axis_size("fine")
    assert amplitudes.shape[0] == 1 and lax.axis_size("coarse") == 2
    assert order & (order - 1) == 0 and order >= 4
    place = jnp.stack([lax.axis_index("coarse"), lax.axis_index("fine")]).astype(jnp.int32)
    square, half = pltpu.VMEM((m, m), f32), pltpu.VMEM((m, m), bf16)
    full = pltpu.VMEM((m, m), f32)
    short = order <= 8

    def params(mib):
        return pltpu.CompilerParams(vmem_limit_bytes=mib << 20)

    def cost(products):
        return pl.CostEstimate(
            flops=6 * products * m**3, bytes_accessed=12 * products * m * m, transcendentals=0
        )

    rows = lax.optimization_barrier(jnp.concatenate([amplitudes, control_index.astype(f32)], axis=1))
    bit, parts = 1, []
    while bit < order:
        swap = [(i, i ^ bit) for i in range(order)]
        coming = lax.ppermute(rows, "fine", swap)
        if bit == 1:
            table, wh, wl = pl.pallas_call(
                first_kernel,
                out_shape=(pltpu.VMEM((kinds + 1, m, m), f32), half, half),
                in_specs=[SMEM, HBM, HBM],
                out_specs=(VMEM, VMEM, VMEM),
                scratch_shapes=[
                    pltpu.VMEM((count + 1, m, m), f32), *Work.shapes(m),
                    pltpu.SemaphoreType.DMA((count + kinds + 2,)),
                ],
                compiler_params=params(FIRST_MIB),
                cost_estimate=cost(4),
                name="first",
            )(rows, outside(controls), outside(drift_term))
        elif bit == 2:
            th, tl, table = pl.pallas_call(
                flip_kernel,
                out_shape=(half, half, pltpu.VMEM((kinds + 1, m, m), f32)),
                in_specs=[SMEM, VMEM, VMEM],
                out_specs=(VMEM, VMEM, VMEM),
                input_output_aliases={2: 2},
                compiler_params=params(TURN_MIB),
                cost_estimate=cost(1),
                name="flip",
            )(rows, target, inside(table))
        rows = jnp.concatenate([rows, coming], axis=0)
        bit *= 2

    outs = (square, square)
    if short:
        kernel, taken = chain_kernel, (rows, table, wh, wl)
        scratch = [half, half, full] + [half] * 4 + [full, half, half, full, half, half, half, half] * 2
    else:
        kernel, taken = long_kernel, (rows, table)
        scratch = [pltpu.VMEM((2, m, m), bf16)] * 2 + [half] * 2 + Work.shapes(m) * 2
    run, local = pl.pallas_call(
        functools.partial(kernel, order),
        out_shape=outs,
        in_specs=[SMEM, SMEM] + [VMEM] * (len(taken) - 1),
        out_specs=(VMEM,) * len(outs),
        scratch_shapes=scratch,
        compiler_params=params(CHAIN_MIB),
        cost_estimate=cost(23),
        name="chain",
    )(place, taken[0], *map(inside, taken[1:]))
    got = lax.ppermute(run, "coarse", [(0, 1), (1, 0)])
    turned = pl.pallas_call(
        target_kernel,
        out_shape=square,
        in_specs=[VMEM, VMEM, VMEM],
        out_specs=VMEM,
        scratch_shapes=[half] * 2,
        compiler_params=params(TURN_MIB),
        cost_estimate=cost(1),
        name="turn",
    )(run, inside(th), inside(tl))
    return pl.pallas_call(
        functools.partial(final_kernel, count),
        out_shape=jax.ShapeDtypeStruct((1, count), f32),
        in_specs=[SMEM, SMEM] + [VMEM] * 7,
        out_specs=SMEM,
        scratch_shapes=[half, half, half, half, half, half, full, half, half, half, half, full],
        compiler_params=params(FINAL_MIB),
        name="final",
    )(place, control_index, run, got, *map(inside, (turned, th, tl, local, table)))


FIRST_MIB = 16
CHAIN_MIB = 22
TURN_MIB = 6
FINAL_MIB = 12


def solution(mesh):
    placed = (
        P(("groups", "coarse", "fine"), None),
        P(("groups", "coarse", "fine"), None),
        P(),
        P(),
        P("groups", None),
    )
    return jax.shard_map(
        on_device,
        mesh=mesh,
        in_specs=placed,
        out_specs=P(("groups", "coarse", "fine"), None),
        check_vma=False,
    )
```

```python
import functools

import jax
import jax.numpy as jnp
from jax import lax
from jax.experimental import pallas as pl
from jax.experimental.pallas import tpu as pltpu
from jax.sharding import PartitionSpec as P

step_scale = 0.3
f32 = jnp.float32
bf16 = jnp.bfloat16
SMEM = pl.BlockSpec(memory_space=pltpu.SMEM)
VMEM = pl.BlockSpec(memory_space=pltpu.VMEM)
HBM = pl.BlockSpec(memory_space=pltpu.HBM)


def split(x):
    high = x.astype(bf16)
    return high, (x - high.astype(f32)).astype(bf16)


def dot(a, b):
    return jnp.dot(a, b, preferred_element_type=f32)


def dot_nt(a, b):
    return lax.dot_general(a, b, (((1,), (1,)), ((), ())), preferred_element_type=f32)


def pieces(m, size):
    size = size if m % size == 0 else m
    return [slice(at, at + size) for at in range(0, m, size)]


def dot3(ah, al, bh, bl, cols, rows=slice(None)):
    return (
        dot(ah[rows, :], bh[:, cols])
        + dot(ah[rows, :], bl[:, cols])
        + dot(al[rows, :], bh[:, cols])
    )


def skewed(ref):
    m = ref.shape[0]
    for i, ti in enumerate(pieces(m, 128)):
        for tj in pieces(m, 128)[: i + 1]:
            value = (step_scale * 0.5) * (ref[ti, tj] - ref[tj, ti].T)
            ref[ti, tj] = value
            if ti != tj:
                ref[tj, ti] = -value.T


def generator(amps, picks, table, s):
    kinds = table.shape[0] - 1
    m = table.shape[1]
    for i, ti in enumerate(pieces(m, 128)):
        for tj in pieces(m, 128)[: i + 1]:
            value = table[kinds, ti, tj]
            for amp, pick in zip(amps, picks):
                value = value + amp * table[pick, ti, tj]
            s.a32[ti, tj] = value
            s.ah[ti, tj], s.al[ti, tj] = split(value)
            if ti != tj:
                back = -value.T
                s.a32[tj, ti] = back
                s.ah[tj, ti], s.al[tj, ti] = split(back)


def mirrored(ah, al, bh, bl, sign, put):
    m = ah.shape[0]
    for cs in pieces(m, 256):
        value = dot3(ah, al, bh, bl, cs, slice(cs.start, m))
        put(slice(cs.start, m), cs, value)
        width = cs.stop - cs.start
        for rs in pieces(m, 256):
            if rs.start > cs.start:
                at = rs.start - cs.start
                flipped = value[at : at + width, :].T
                put(cs, rs, flipped if sign > 0 else -flipped)


def square_step(s):
    def put(rows, cols, value):
        s.b32[rows, cols] = value
        s.bh[rows, cols], s.bl[rows, cols] = split(value)

    mirrored(s.ah, s.al, s.ah, s.al, 1, put)


def cube_step(s):
    def put(rows, cols, value):
        s.dh[rows, cols], s.dl[rows, cols] = split(value)
        a, b = s.a32[rows, cols], s.b32[rows, cols]
        rest = a * (1 / 24) + b * (1 / 120) + value * (1 / 720)
        s.qh[rows, cols], s.ql[rows, cols] = split(rest)
        s.a32[rows, cols] = a + b * 0.5 + value * (1 / 6)

    mirrored(s.ah, s.al, s.bh, s.bl, -1, put)


def last_step(s, wh, wl):
    for cs in pieces(s.ah.shape[0], 256):
        value = dot3(s.dh, s.dl, s.qh, s.ql, cs) + s.a32[:, cs]
        wh[:, cs], wl[:, cs] = split(value)


def inside(x):
    return pltpu.with_memory_space_constraint(x, pltpu.VMEM)


def outside(x):
    return pltpu.with_memory_space_constraint(x, pltpu.HBM)


class Work:
    names = ("a32", "b32", "ah", "al", "bh", "bl", "dh", "dl", "qh", "ql")

    def __init__(self, refs):
        for name, ref in zip(self.names, refs):
            setattr(self, name, ref)

    @classmethod
    def shapes(cls, m):
        return [pltpu.VMEM((m, m), f32)] * 2 + [pltpu.VMEM((m, m), bf16)] * 8


def propagators(rows, picked, table, works, wh, wl, first):
    count = rows.shape[1] // 2
    for row, s in zip(picked, works):
        amps = [rows[row, c] for c in range(count)]
        picks = [rows[row, count + c].astype(jnp.int32) for c in range(count)]
        generator(amps, picks, table, s)
    for s in works:
        square_step(s)
    for s in works:
        cube_step(s)
    for k, (row, s) in enumerate(zip(picked, works)):
        slot = k if first is None else first + row
        last_step(s, wh.at[slot], wl.at[slot])


def load_kernel(controls, drift, table, sems):
    kinds = controls.shape[0]

    def copy(k):
        return pltpu.make_async_copy(controls.at[k], table.at[k], sems.at[k])

    last = pltpu.make_async_copy(drift, table.at[kinds], sems.at[kinds])
    for k in range(kinds):
        copy(k).start()
    last.start()

    def one(k, carry):
        copy(k).wait()
        skewed(table.at[k])
        return carry

    lax.fori_loop(0, kinds, one, 0)
    last.wait()
    skewed(table.at[kinds])


def build_kernel(first, rows, table, *refs):
    wh, wl = refs[-2 - 2 * len(Work.names) : -2 * len(Work.names)]
    scratch = refs[-2 * len(Work.names) :]
    size = len(Work.names)
    slots = rows.shape[0]
    works = [Work(scratch[n * size : (n + 1) * size]) for n in range(len(scratch) // size)]
    for n in range(0, slots, len(works)):
        propagators(rows, range(n, n + len(works)), table, works, wh, wl, first)


def chain_kernel(order, place, rows, table, wh_in, wl_in, run, local, wh, wl, rh, rl, both, *scratch):
    size = len(Work.names)
    works = [Work(scratch[n * size : (n + 1) * size]) for n in range(2)]
    m = run.shape[0]
    fine = place[1]
    first = order - rows.shape[0]

    def pair(n, carry):
        propagators(rows, [2 * n, 2 * n + 1], table, works, wh, wl, first)
        return carry

    lax.fori_loop(0, rows.shape[0] // 2, pair, 0)
    start_product(fine, wh.at[fine], wl.at[fine], run, rh, rl)
    for rs in pieces(m, 32):
        both[0, rs, :] = run[rs, :]
    for step in range(1, order):
        slot = step ^ fine
        side = jnp.where(step <= fine, 0, 1)
        for cs in pieces(m, 256):
            value = dot3(wh.at[slot], wl.at[slot], rh, rl, cs) + run[:, cs]
            run[:, cs] = value
            both[side, :, cs] = value
            rh[:, cs], rl[:, cs] = split(value)
    for rs in pieces(m, 32):
        local[rs, :] = both[0, rs, :]


def long_kernel(order, place, rows, table, run, local, wh, wl, rh, rl, *scratch):
    size = len(Work.names)
    works = [Work(scratch[n * size : (n + 1) * size]) for n in range(2)]
    m = run.shape[0]
    fine = place[1]
    for rs in pieces(m, 32):
        value = unit(rs, m)
        run[rs, :] = value
        rh[rs, :], rl[rs, :] = split(value)

    def pair(n, carry):
        steps = [2 * n, 2 * n + 1]
        propagators(rows, [step ^ fine for step in steps], table, works, wh, wl, None)
        for k, step in enumerate(steps):
            for cs in pieces(m, 256):
                value = dot3(wh.at[k], wl.at[k], rh, rl, cs) + run[:, cs]
                run[:, cs] = value
                rh[:, cs], rl[:, cs] = split(value)

            @pl.when(step == fine)
            def _():
                for rs in pieces(m, 32):
                    local[rs, :] = run[rs, :]

        return carry

    lax.fori_loop(0, order // 2, pair, 0)


def unit(rs, m):
    at = lax.broadcasted_iota(jnp.int32, (rs.stop - rs.start, m), 0) + rs.start
    return (at == lax.broadcasted_iota(jnp.int32, (rs.stop - rs.start, m), 1)).astype(f32)


def start_product(fine, wh, wl, run, rh, rl):
    m = run.shape[0]
    for rs in pieces(m, 32):
        value = wh[rs, :].astype(f32) + wl[rs, :].astype(f32) + unit(rs, m)
        run[rs, :] = value
        rh[rs, :], rl[rs, :] = split(value)


def turn_kernel(run, local, target, vh, vl, bh, bl, ph, plo, th, tl):
    m = run.shape[0]
    for ti in pieces(m, 128):
        bh[ti, :], bl[ti, :] = split(run[ti, :])
        for tj in pieces(m, 128):
            th[ti, tj], tl[ti, tj] = split(target[tj, ti].T)
    for cs in pieces(m, 256):
        vh[:, cs], vl[:, cs] = split(dot3(th, tl, bh, bl, cs))
    for rs in pieces(m, 32):
        ph[rs, :], plo[rs, :] = split(local[rs, :])


def final_kernel(
    count, place, picks, got, turned_h, turned_l, run_h, run_l, local_h, local_l, th, tl, table, out,
    gh, gl, ph, plo, vh, vl, x32, kh, kl, uh, ul,
):
    m = got.shape[0]
    coarse = place[0]
    for rs in pieces(m, 32):
        gh[rs, :], gl[rs, :] = split(got[rs, :])

    @pl.when(coarse == 0)
    def _():
        for rs in pieces(m, 64):
            ph[rs, :], plo[rs, :] = local_h[rs, :], local_l[rs, :]
        for cs in pieces(m, 256):
            vh[:, cs], vl[:, cs] = split(dot3(th, tl, gh, gl, cs))
        for cs in pieces(m, 256):
            x32[:, cs] = dot3(vh, vl, run_h, run_l, cs)

    @pl.when(coarse != 0)
    def _():
        for cs in pieces(m, 256):
            x32[:, cs] = dot3(turned_h, turned_l, gh, gl, cs)
        for cs in pieces(m, 256):
            ph[:, cs], plo[:, cs] = split(dot3(local_h, local_l, gh, gl, cs))

    for i, ti in enumerate(pieces(m, 128)):
        for tj in pieces(m, 128)[: i + 1]:
            value = 0.5 * (x32[tj, ti].T - x32[ti, tj])
            kh[ti, tj], kl[ti, tj] = split(value)
            if ti != tj:
                kh[tj, ti], kl[tj, ti] = split(-value.T)
    for cs in pieces(m, 256):
        uh[:, cs], ul[:, cs] = split(dot3(ph, plo, kh, kl, cs))
    totals = [None] * count
    for cs in pieces(m, 256):
        for rs in pieces(m, 256):
            if rs.start < cs.start:
                continue
            value = (
                dot_nt(uh[rs, :], ph[cs, :]) + dot_nt(uh[rs, :], plo[cs, :]) + dot_nt(ul[rs, :], ph[cs, :])
            )
            for c in range(count):
                part = jnp.sum(table[picks[0, c], rs, cs] * value, axis=0, keepdims=True)
                if rs.start > cs.start:
                    part = part * 2.0
                totals[c] = part if totals[c] is None else totals[c] + part
    for c in range(count):
        out[0, c] = jnp.sum(totals[c])


def on_device(amplitudes, control_index, controls, drift_term, target):
    m = target.shape[0]
    kinds, count = controls.shape[0], amplitudes.shape[1]
    order = lax.axis_size("fine")
    assert amplitudes.shape[0] == 1 and lax.axis_size("coarse") == 2
    assert order & (order - 1) == 0 and order >= 4
    place = jnp.stack([lax.axis_index("coarse"), lax.axis_index("fine")]).astype(jnp.int32)
    square, half = pltpu.VMEM((m, m), f32), pltpu.VMEM((m, m), bf16)
    full = pltpu.VMEM((m, m), f32)
    short = order <= 8

    def params(mib):
        return pltpu.CompilerParams(vmem_limit_bytes=mib << 20)

    def cost(products):
        return pl.CostEstimate(
            flops=6 * products * m**3, bytes_accessed=12 * products * m * m, transcendentals=0
        )

    rows = lax.optimization_barrier(jnp.concatenate([amplitudes, control_index.astype(f32)], axis=1))
    wh = wl = coming = None
    bit = 1
    while bit < order:
        swap = [(i, i ^ bit) for i in range(order)]
        fresh = rows if bit == 2 else coming
        coming = lax.ppermute(rows, "fine", swap)
        if bit == 1:
            table = pl.pallas_call(
                load_kernel,
                out_shape=pltpu.VMEM((kinds + 1, m, m), f32),
                in_specs=[HBM, HBM],
                out_specs=VMEM,
                scratch_shapes=[pltpu.SemaphoreType.DMA((kinds + 1,))],
                compiler_params=params(LOAD_MIB),
                cost_estimate=cost(2),
                name="load",
            )(outside(controls), outside(drift_term))
        elif short:
            past = () if wh is None else (inside(wh), inside(wl))
            wh, wl = pl.pallas_call(
                functools.partial(build_kernel, bit - fresh.shape[0]),
                out_shape=(pltpu.VMEM((order, m, m), bf16),) * 2,
                in_specs=[SMEM, VMEM] + [VMEM] * len(past),
                out_specs=(VMEM, VMEM),
                scratch_shapes=Work.shapes(m) * 2,
                input_output_aliases={2: 0, 3: 1} if past else {},
                compiler_params=params(BUILD_MIB),
                cost_estimate=cost(4 * fresh.shape[0]),
                name="build",
            )(fresh, inside(table), *past)
        rows = jnp.concatenate([rows, coming], axis=0)
        bit *= 2

    if short:
        kernel, taken = chain_kernel, (coming, table, wh, wl)
        outs, aliases = (square, square) + (pltpu.VMEM((order, m, m), bf16),) * 2, {3: 2, 4: 3}
        scratch = [half, half, pltpu.VMEM((2, m, m), f32)]
    else:
        kernel, taken = long_kernel, (rows, table)
        outs, aliases = (square, square), {}
        scratch = [pltpu.VMEM((2, m, m), bf16), pltpu.VMEM((2, m, m), bf16), half, half]
    run, local = pl.pallas_call(
        functools.partial(kernel, order),
        out_shape=outs,
        in_specs=[SMEM, SMEM] + [VMEM] * (len(taken) - 1),
        out_specs=(VMEM,) * len(outs),
        scratch_shapes=[*scratch, *Work.shapes(m) * 2],
        input_output_aliases=aliases,
        compiler_params=params(CHAIN_MIB),
        cost_estimate=cost(23),
        name="chain",
    )(place, taken[0], *map(inside, taken[1:]))[:2]
    got = lax.ppermute(run, "coarse", [(0, 1), (1, 0)])
    turned = pl.pallas_call(
        turn_kernel,
        out_shape=(half,) * 8,
        in_specs=[VMEM] * 3,
        out_specs=(VMEM,) * 8,
        compiler_params=params(TURN_MIB),
        cost_estimate=cost(1),
        name="turn",
    )(inside(run), inside(local), target)
    return pl.pallas_call(
        functools.partial(final_kernel, count),
        out_shape=jax.ShapeDtypeStruct((1, count), f32),
        in_specs=[SMEM, SMEM] + [VMEM] * 10,
        out_specs=SMEM,
        scratch_shapes=[half] * 6 + [full] + [half] * 4,
        compiler_params=params(FINAL_MIB),
        name="final",
    )(place, control_index, got, *map(inside, (*turned, table)))


LOAD_MIB = 4
BUILD_MIB = 14
CHAIN_MIB = 20
TURN_MIB = 6
FINAL_MIB = 12


def solution(mesh):
    placed = (
        P(("groups", "coarse", "fine"), None),
        P(("groups", "coarse", "fine"), None),
        P(),
        P(),
        P("groups", None),
    )
    return jax.shard_map(
        on_device,
        mesh=mesh,
        in_specs=placed,
        out_specs=P(("groups", "coarse", "fine"), None),
        check_vma=False,
    )
```

```python
import functools

import jax
import jax.numpy as jnp
from jax import lax
from jax.experimental import pallas as pl
from jax.experimental.pallas import tpu as pltpu
from jax.sharding import PartitionSpec as P

step_scale = 0.3
f32 = jnp.float32
bf16 = jnp.bfloat16
SMEM = pl.BlockSpec(memory_space=pltpu.SMEM)
VMEM = pl.BlockSpec(memory_space=pltpu.VMEM)
HBM = pl.BlockSpec(memory_space=pltpu.HBM)


def split(x):
    high = x.astype(bf16)
    return high, (x - high.astype(f32)).astype(bf16)


def dot(a, b):
    return jnp.dot(a, b, preferred_element_type=f32)


def dot_nt(a, b):
    return lax.dot_general(a, b, (((1,), (1,)), ((), ())), preferred_element_type=f32)


def pieces(m, size):
    size = size if m % size == 0 else m
    return [slice(at, at + size) for at in range(0, m, size)]


def dot3(ah, al, bh, bl, cols, rows=slice(None)):
    return (
        dot(ah[rows, :], bh[:, cols])
        + dot(ah[rows, :], bl[:, cols])
        + dot(al[rows, :], bh[:, cols])
    )


def lower_tiles(m):
    return [(ti, tj) for i, ti in enumerate(pieces(m, 128)) for tj in pieces(m, 128)[: i + 1]]


def skewed(ref):
    for ti, tj in lower_tiles(ref.shape[0]):
        ref[ti, tj] = (step_scale * 0.5) * (ref[ti, tj] - ref[tj, ti].T)


def generator(amps, picks, table, s):
    kinds = table.shape[0] - 1
    for ti, tj in lower_tiles(table.shape[1]):
        value = table[kinds, ti, tj]
        for amp, pick in zip(amps, picks):
            value = value + amp * table[pick, ti, tj]
        s.a32[ti, tj] = value
        s.ah[ti, tj], s.al[ti, tj] = split(value)
        if ti != tj:
            back = -value.T
            s.a32[tj, ti] = back
            s.ah[tj, ti], s.al[tj, ti] = split(back)


def mirrored(ah, al, bh, bl, sign, put):
    m = ah.shape[0]
    for cs in pieces(m, 256):
        value = dot3(ah, al, bh, bl, cs, slice(cs.start, m))
        put(slice(cs.start, m), cs, value)
        width = cs.stop - cs.start
        for rs in pieces(m, 256):
            if rs.start > cs.start:
                at = rs.start - cs.start
                flipped = value[at : at + width, :].T
                put(cs, rs, flipped if sign > 0 else -flipped)


def square_step(s):
    def put(rows, cols, value):
        s.b32[rows, cols] = value
        s.bh[rows, cols], s.bl[rows, cols] = split(value)

    mirrored(s.ah, s.al, s.ah, s.al, 1, put)


def cube_step(s):
    def put(rows, cols, value):
        s.dh[rows, cols], s.dl[rows, cols] = split(value)
        a, b = s.a32[rows, cols], s.b32[rows, cols]
        rest = a * (1 / 24) + b * (1 / 120) + value * (1 / 720)
        s.qh[rows, cols], s.ql[rows, cols] = split(rest)
        s.a32[rows, cols] = a + b * 0.5 + value * (1 / 6)

    mirrored(s.ah, s.al, s.bh, s.bl, -1, put)


def last_step(s, wh, wl):
    m = s.ah.shape[0]
    for cs in pieces(m, 256):
        value = dot3(s.dh, s.dl, s.qh, s.ql, cs) + s.a32[:, cs]
        for rs in pieces(m, 256):
            part = value[rs, :]
            if rs == cs:
                part = part + unit(part.shape)
            wh[rs, cs], wl[rs, cs] = split(part)


def unit(shape):
    return (
        lax.broadcasted_iota(jnp.int32, shape, 0) == lax.broadcasted_iota(jnp.int32, shape, 1)
    ).astype(f32)


def inside(x):
    return pltpu.with_memory_space_constraint(x, pltpu.VMEM)


def outside(x):
    return pltpu.with_memory_space_constraint(x, pltpu.HBM)


class Work:
    names = ("a32", "b32", "ah", "al", "bh", "bl", "dh", "dl", "qh", "ql")

    def __init__(self, refs):
        for name, ref in zip(self.names, refs):
            setattr(self, name, ref)

    @classmethod
    def shapes(cls, m):
        return [pltpu.VMEM((m, m), f32)] * 2 + [pltpu.VMEM((m, m), bf16)] * 8


def propagators(rows, picked, table, works, wh, wl, first):
    count = rows.shape[1] // 2
    for row, s in zip(picked, works):
        amps = [rows[row, c] for c in range(count)]
        picks = [rows[row, count + c].astype(jnp.int32) for c in range(count)]
        generator(amps, picks, table, s)
    for s in works:
        square_step(s)
    for s in works:
        cube_step(s)
    for k, (row, s) in enumerate(zip(picked, works)):
        slot = k if first is None else first + row
        last_step(s, wh.at[slot], wl.at[slot])


def load_kernel(controls, drift, table, sems):
    kinds = controls.shape[0]

    def copy(k):
        return pltpu.make_async_copy(controls.at[k], table.at[k], sems.at[k])

    last = pltpu.make_async_copy(drift, table.at[kinds], sems.at[kinds])
    for k in range(kinds):
        copy(k).start()
    last.start()

    waits = [copy(k) for k in range(kinds)] + [last]
    for at in range(0, kinds + 1, 3):
        group = range(at, min(at + 3, kinds + 1))
        for k in group:
            waits[k].wait()
        for k in group:
            skewed(table.at[k])


def build_kernel(first, rows, table, *refs):
    size = len(Work.names)
    width = rows.shape[0]
    wh, wl = refs[-2 - width * size : -width * size]
    scratch = refs[-width * size :]
    works = [Work(scratch[n * size : (n + 1) * size]) for n in range(width)]
    propagators(rows, range(width), table, works, wh, wl, first)


def join(run, wh, wl, rh, rl):
    for cs in pieces(rh.shape[0], 256):
        value = dot3(wh, wl, rh, rl, cs)
        if run is not None:
            run[:, cs] = value
        yield cs, split(value)


def chain_kernel(order, place, rows, table, wh_in, wl_in, run, lh, ll, wh, wl, rh, rl, bh, bl, *scratch):
    size = len(Work.names)
    works = [Work(scratch[n * size : (n + 1) * size]) for n in range(2)]
    m = run.shape[0]
    fine = place[1]
    first = order - rows.shape[0]

    def pair(n, carry):
        propagators(rows, [2 * n, 2 * n + 1], table, works, wh, wl, first)
        return carry

    lax.fori_loop(0, rows.shape[0] // 2, pair, 0)
    for rs in pieces(m, 64):
        high, low = wh[fine, rs, :], wl[fine, rs, :]
        rh[rs, :], rl[rs, :] = high, low
        bh[0, rs, :], bl[0, rs, :] = high, low
    for step in range(1, order):
        slot = step ^ fine
        side = jnp.where(step <= fine, 0, 1)
        for cs, (high, low) in join(run if step == order - 1 else None, wh.at[slot], wl.at[slot], rh, rl):
            rh[:, cs], rl[:, cs] = high, low
            bh[side, :, cs], bl[side, :, cs] = high, low
    for rs in pieces(m, 64):
        lh[rs, :], ll[rs, :] = bh[0, rs, :], bl[0, rs, :]


def long_kernel(order, place, rows, table, run, lh, ll, wh, wl, rh, rl, *scratch):
    size = len(Work.names)
    works = [Work(scratch[n * size : (n + 1) * size]) for n in range(2)]
    m = run.shape[0]
    fine = place[1]
    for rs in pieces(m, 256):
        for cs in pieces(m, 256):
            shape = (rs.stop - rs.start, cs.stop - cs.start)
            rh[rs, cs], rl[rs, cs] = split(unit(shape) if rs == cs else jnp.zeros(shape, f32))

    def pair(n, carry):
        steps = [2 * n, 2 * n + 1]
        propagators(rows, [step ^ fine for step in steps], table, works, wh, wl, None)
        for k, step in enumerate(steps):
            for cs, (high, low) in join(run, wh.at[k], wl.at[k], rh, rl):
                rh[:, cs], rl[:, cs] = high, low

            @pl.when(step == fine)
            def _():
                for rs in pieces(m, 64):
                    lh[rs, :], ll[rs, :] = rh[rs, :], rl[rs, :]

        return carry

    lax.fori_loop(0, order // 2, pair, 0)


def turn_kernel(run, target, vh, vl, bh, bl, th, tl):
    m = run.shape[0]
    for ti in pieces(m, 128):
        bh[ti, :], bl[ti, :] = split(run[ti, :])
        for tj in pieces(m, 128):
            th[ti, tj], tl[ti, tj] = split(target[tj, ti].T)
    for cs in pieces(m, 256):
        vh[:, cs], vl[:, cs] = split(dot3(th, tl, bh, bl, cs))


def final_kernel(
    count, place, picks, got, turned_h, turned_l, run_h, run_l, local_h, local_l, th, tl, table, out,
    gh, gl, ph, plo, vh, vl, x32, kh, kl, uh, ul,
):
    m = got.shape[0]
    coarse = place[0]
    for rs in pieces(m, 32):
        gh[rs, :], gl[rs, :] = split(got[rs, :])

    @pl.when(coarse == 0)
    def _():
        for rs in pieces(m, 64):
            ph[rs, :], plo[rs, :] = local_h[rs, :], local_l[rs, :]
        for cs in pieces(m, 256):
            vh[:, cs], vl[:, cs] = split(dot3(th, tl, gh, gl, cs))
        for cs in pieces(m, 256):
            x32[:, cs] = dot3(vh, vl, run_h, run_l, cs)

    @pl.when(coarse != 0)
    def _():
        for cs in pieces(m, 256):
            x32[:, cs] = dot3(turned_h, turned_l, gh, gl, cs)
        for cs in pieces(m, 256):
            ph[:, cs], plo[:, cs] = split(dot3(local_h, local_l, gh, gl, cs))

    for i, ti in enumerate(pieces(m, 128)):
        for tj in pieces(m, 128)[: i + 1]:
            value = 0.5 * (x32[tj, ti].T - x32[ti, tj])
            kh[ti, tj], kl[ti, tj] = split(value)
            if ti != tj:
                kh[tj, ti], kl[tj, ti] = split(-value.T)
    for cs in pieces(m, 256):
        uh[:, cs], ul[:, cs] = split(dot3(ph, plo, kh, kl, cs))
    totals = [jnp.zeros((8, 128), f32)] * count
    for cs in pieces(m, 256):
        for rs in pieces(m, 256):
            if rs.start < cs.start:
                continue
            value = (
                dot_nt(uh[rs, :], ph[cs, :]) + dot_nt(uh[rs, :], plo[cs, :]) + dot_nt(ul[rs, :], ph[cs, :])
            )
            for ti, tj in lower_tiles(m):
                if not (rs.start <= ti.start < rs.stop and cs.start <= tj.start < cs.stop):
                    continue
                tile = value[ti.start - rs.start : ti.stop - rs.start, tj.start - cs.start : tj.stop - cs.start]
                if ti != tj:
                    tile = tile + tile
                for c in range(count):
                    part = table[picks[0, c], ti, tj] * tile
                    for at in range(0, part.shape[0], 8):
                        totals[c] = totals[c] + part[at : at + 8, :]
    for c in range(count):
        out[0, c] = jnp.sum(totals[c])


def on_device(amplitudes, control_index, controls, drift_term, target):
    m = target.shape[0]
    kinds, count = controls.shape[0], amplitudes.shape[1]
    order = lax.axis_size("fine")
    assert amplitudes.shape[0] == 1 and lax.axis_size("coarse") == 2
    assert order & (order - 1) == 0 and order >= 4
    place = jnp.stack([lax.axis_index("coarse"), lax.axis_index("fine")]).astype(jnp.int32)
    square, half = pltpu.VMEM((m, m), f32), pltpu.VMEM((m, m), bf16)
    full = pltpu.VMEM((m, m), f32)
    short = order <= 8

    def params(mib):
        return pltpu.CompilerParams(vmem_limit_bytes=mib << 20)

    def cost(products):
        return pl.CostEstimate(
            flops=6 * products * m**3, bytes_accessed=12 * products * m * m, transcendentals=0
        )

    wh = wl = coming = rows = None
    bit = 1
    while bit < order:
        swap = [(i, i ^ bit) for i in range(order)]
        fresh = rows if bit == 2 else coming
        if bit > 1:
            coming = lax.ppermute(rows, "fine", swap)
            rows_next = (rows, coming)
        else:
            both = lax.ppermute((amplitudes, control_index), "fine", swap)
            rows_next = [
                jnp.concatenate([amps, picks.astype(f32)], axis=1)
                for amps, picks in ((amplitudes, control_index), both)
            ]
            table = pl.pallas_call(
                load_kernel,
                out_shape=pltpu.VMEM((kinds + 1, m, m), f32),
                in_specs=[HBM, HBM],
                out_specs=VMEM,
                scratch_shapes=[pltpu.SemaphoreType.DMA((kinds + 1,))],
                compiler_params=params(LOAD_MIB),
                cost_estimate=cost(2),
                name="load",
            )(outside(controls), outside(drift_term))
        if bit > 1 and short:
            past = () if wh is None else (inside(wh), inside(wl))
            wh, wl = pl.pallas_call(
                functools.partial(build_kernel, bit - fresh.shape[0]),
                out_shape=(pltpu.VMEM((order, m, m), bf16),) * 2,
                in_specs=[SMEM, VMEM] + [VMEM] * len(past),
                out_specs=(VMEM, VMEM),
                scratch_shapes=Work.shapes(m) * 2,
                input_output_aliases={2: 0, 3: 1} if past else {},
                compiler_params=params(BUILD_MIB),
                cost_estimate=cost(4 * fresh.shape[0]),
                name="build",
            )(fresh, inside(table), *past)
        rows = jnp.concatenate(rows_next, axis=0)
        bit *= 2

    if short:
        kernel, taken = chain_kernel, (coming, table, wh, wl)
        outs, aliases = (square, half, half) + (pltpu.VMEM((order, m, m), bf16),) * 2, {3: 3, 4: 4}
        scratch = [half, half] + [pltpu.VMEM((2, m, m), bf16)] * 2
    else:
        kernel, taken = long_kernel, (rows, table)
        outs, aliases = (square, half, half), {}
        scratch = [pltpu.VMEM((2, m, m), bf16), pltpu.VMEM((2, m, m), bf16), half, half]
    run, lh, ll = pl.pallas_call(
        functools.partial(kernel, order),
        out_shape=outs,
        in_specs=[SMEM, SMEM] + [VMEM] * (len(taken) - 1),
        out_specs=(VMEM,) * len(outs),
        scratch_shapes=[*scratch, *Work.shapes(m) * 2],
        input_output_aliases=aliases,
        compiler_params=params(CHAIN_MIB),
        cost_estimate=cost(23),
        name="chain",
    )(place, taken[0], *map(inside, taken[1:]))[:3]
    got = lax.ppermute(run, "coarse", [(0, 1), (1, 0)])
    turned = pl.pallas_call(
        turn_kernel,
        out_shape=(half,) * 6,
        in_specs=[VMEM] * 2,
        out_specs=(VMEM,) * 6,
        compiler_params=params(TURN_MIB),
        cost_estimate=cost(1),
        name="turn",
    )(inside(run), target)
    return pl.pallas_call(
        functools.partial(final_kernel, count),
        out_shape=jax.ShapeDtypeStruct((1, count), f32),
        in_specs=[SMEM, SMEM] + [VMEM] * 10,
        out_specs=SMEM,
        scratch_shapes=[half] * 6 + [full] + [half] * 4,
        compiler_params=params(FINAL_MIB),
        name="final",
    )(place, control_index, got, *map(inside, (*turned[:4], lh, ll, *turned[4:], table)))


LOAD_MIB = 4
BUILD_MIB = 14
CHAIN_MIB = 20
TURN_MIB = 6
FINAL_MIB = 12


def solution(mesh):
    placed = (
        P(("groups", "coarse", "fine"), None),
        P(("groups", "coarse", "fine"), None),
        P(),
        P(),
        P("groups", None),
    )
    return jax.shard_map(
        on_device,
        mesh=mesh,
        in_specs=placed,
        out_specs=P(("groups", "coarse", "fine"), None),
        check_vma=False,
    )
```

```python
import functools

import jax
import jax.numpy as jnp
from jax import lax
from jax.experimental import pallas as pl
from jax.experimental.pallas import tpu as pltpu
from jax.sharding import PartitionSpec as P

step_scale = 0.3
f32 = jnp.float32
bf16 = jnp.bfloat16
SMEM = pl.BlockSpec(memory_space=pltpu.SMEM)
VMEM = pl.BlockSpec(memory_space=pltpu.VMEM)
HBM = pl.BlockSpec(memory_space=pltpu.HBM)


def split(x):
    high = x.astype(bf16)
    return high, (x - high.astype(f32)).astype(bf16)


def dot(a, b):
    return jnp.dot(a, b, preferred_element_type=f32)


def dot_nt(a, b):
    return lax.dot_general(a, b, (((1,), (1,)), ((), ())), preferred_element_type=f32)


def pieces(m, size):
    size = size if m % size == 0 else m
    return [slice(at, at + size) for at in range(0, m, size)]


def dot3(ah, al, bh, bl, cols, rows=slice(None)):
    return (
        dot(ah[rows, :], bh[:, cols])
        + dot(ah[rows, :], bl[:, cols])
        + dot(al[rows, :], bh[:, cols])
    )


def lower_tiles(m):
    return [(ti, tj) for i, ti in enumerate(pieces(m, 128)) for tj in pieces(m, 128)[: i + 1]]


def skewed(ref):
    for ti, tj in lower_tiles(ref.shape[0]):
        ref[ti, tj] = (step_scale * 0.5) * (ref[ti, tj] - ref[tj, ti].T)


def generator(amps, picks, table, s):
    kinds = table.shape[0] - 1
    for ti, tj in lower_tiles(table.shape[1]):
        value = table[kinds, ti, tj]
        for amp, pick in zip(amps, picks):
            value = value + amp * table[pick, ti, tj]
        s.a32[ti, tj] = value
        s.ah[ti, tj], s.al[ti, tj] = split(value)
        if ti != tj:
            back = -value.T
            s.a32[tj, ti] = back
            s.ah[tj, ti], s.al[tj, ti] = split(back)


def mirrored(ah, al, bh, bl, sign, put):
    m = ah.shape[0]
    for cs in pieces(m, 256):
        value = dot3(ah, al, bh, bl, cs, slice(cs.start, m))
        put(slice(cs.start, m), cs, value)
        width = cs.stop - cs.start
        for rs in pieces(m, 256):
            if rs.start > cs.start:
                at = rs.start - cs.start
                flipped = value[at : at + width, :].T
                put(cs, rs, flipped if sign > 0 else -flipped)


def square_step(s):
    def put(rows, cols, value):
        s.b32[rows, cols] = value
        s.bh[rows, cols], s.bl[rows, cols] = split(value)

    mirrored(s.ah, s.al, s.ah, s.al, 1, put)


def cube_step(s):
    def put(rows, cols, value):
        s.dh[rows, cols], s.dl[rows, cols] = split(value)
        a, b = s.a32[rows, cols], s.b32[rows, cols]
        rest = a * (1 / 24) + b * (1 / 120) + value * (1 / 720)
        s.qh[rows, cols], s.ql[rows, cols] = split(rest)
        s.a32[rows, cols] = a + b * 0.5 + value * (1 / 6)

    mirrored(s.ah, s.al, s.bh, s.bl, -1, put)


def last_step(s, wh, wl):
    m = s.ah.shape[0]
    for cs in pieces(m, 256):
        value = dot3(s.dh, s.dl, s.qh, s.ql, cs) + s.a32[:, cs]
        for rs in pieces(m, 256):
            part = value[rs, :]
            if rs == cs:
                part = part + unit(part.shape)
            wh[rs, cs], wl[rs, cs] = split(part)


def unit(shape):
    return (
        lax.broadcasted_iota(jnp.int32, shape, 0) == lax.broadcasted_iota(jnp.int32, shape, 1)
    ).astype(f32)


def inside(x):
    return pltpu.with_memory_space_constraint(x, pltpu.VMEM)


def outside(x):
    return pltpu.with_memory_space_constraint(x, pltpu.HBM)


class Work:
    names = ("a32", "b32", "ah", "al", "bh", "bl", "dh", "dl", "qh", "ql")

    def __init__(self, refs):
        for name, ref in zip(self.names, refs):
            setattr(self, name, ref)

    @classmethod
    def shapes(cls, m):
        return [pltpu.VMEM((m, m), f32)] * 2 + [pltpu.VMEM((m, m), bf16)] * 8


def propagators(amps, picks, picked, works, table, wh, wl, slots):
    count = amps.shape[1]
    for row, s in zip(picked, works):
        generator([amps[row, c] for c in range(count)], [picks[row, c] for c in range(count)], table, s)
    for s in works:
        square_step(s)
    for s in works:
        cube_step(s)
    for slot, s in zip(slots, works):
        last_step(s, wh.at[slot], wl.at[slot])


def load_kernel(controls, drift, table, sems):
    kinds = controls.shape[0]

    def copy(k):
        return pltpu.make_async_copy(controls.at[k], table.at[k], sems.at[k])

    last = pltpu.make_async_copy(drift, table.at[kinds], sems.at[kinds])
    for k in range(kinds):
        copy(k).start()
    last.start()

    waits = [copy(k) for k in range(kinds)] + [last]
    for at in range(0, kinds + 1, 3):
        group = range(at, min(at + 3, kinds + 1))
        for k in group:
            waits[k].wait()
        for k in group:
            skewed(table.at[k])


def works_of(scratch):
    size = len(Work.names)
    return [Work(scratch[at : at + size]) for at in range(0, len(scratch), size)]


def build_kernel(first, amps, picks, table, *refs):
    size = len(Work.names)
    width = amps.shape[0]
    wh, wl = refs[-2 - width * size : -width * size]
    slots = [first + n for n in range(width)]
    propagators(amps, picks, range(width), works_of(refs[-width * size :]), table, wh, wl, slots)


def multiply(ah, al, bh, bl):
    for cs in pieces(ah.shape[0], 256):
        yield cs, dot3(ah, al, bh, bl, cs)


def chain_kernel(
    place, amps, picks, table, early_h, early_l, run, lh, ll, oh, ol,
    wh, wl, th, tl, qh, ql, bh, bl, *scratch
):
    half, m = early_h.shape[:2]
    fine = place[1]
    inner = fine & (half - 1)
    upper = jnp.where(fine < half, 1, 0)
    propagators(amps, picks, range(half), works_of(scratch), table, wh, wl, range(half))
    for rs in pieces(m, 64):
        high, low = early_h[inner, rs, :], early_l[inner, rs, :]
        qh[0, rs, :], ql[0, rs, :] = high, low
        bh[0, rs, :], bl[0, rs, :] = high, low
    for step in range(1, half):
        slot = step ^ inner
        side = jnp.where(step <= inner, 0, 1)
        for cs, value in multiply(early_h.at[slot], early_l.at[slot], qh.at[0], ql.at[0]):
            high, low = split(value)
            qh[0, :, cs], ql[0, :, cs] = high, low
            bh[side, :, cs], bl[side, :, cs] = high, low
    for rs in pieces(m, 64):
        lh[rs, :], ll[rs, :] = bh[0, rs, :], bl[0, rs, :]
    level = [(wh.at[step ^ inner], wl.at[step ^ inner]) for step in range(half)]
    free = 0
    while len(level) > 1:
        above = []
        for n in range(0, len(level), 2):
            goal = (qh.at[1], ql.at[1]) if len(level) == 2 else (th.at[free], tl.at[free])
            free += 1
            for cs, value in multiply(*level[n + 1], *level[n]):
                goal[0][:, cs], goal[1][:, cs] = split(value)
            above.append(goal)
        level = above
    for cs, value in multiply(qh.at[upper], ql.at[upper], qh.at[1 - upper], ql.at[1 - upper]):
        run[:, cs] = value
    for rs in pieces(m, 64):
        oh[rs, :], ol[rs, :] = qh[1, rs, :], ql[1, rs, :]


def long_kernel(order, place, amps, picks, table, run, lh, ll, wh, wl, rh, rl, *scratch):
    works = works_of(scratch)
    m = run.shape[0]
    fine = place[1]
    for rs in pieces(m, 256):
        for cs in pieces(m, 256):
            shape = (rs.stop - rs.start, cs.stop - cs.start)
            rh[rs, cs], rl[rs, cs] = split(unit(shape) if rs == cs else jnp.zeros(shape, f32))

    def pair(n, carry):
        steps = [2 * n, 2 * n + 1]
        propagators(amps, picks, [step ^ fine for step in steps], works, table, wh, wl, range(2))
        for k, step in enumerate(steps):
            for cs, value in multiply(wh.at[k], wl.at[k], rh, rl):
                run[:, cs] = value
                rh[:, cs], rl[:, cs] = split(value)

            @pl.when(step == fine)
            def _():
                for rs in pieces(m, 64):
                    lh[rs, :], ll[rs, :] = rh[rs, :], rl[rs, :]

        return carry

    lax.fori_loop(0, order // 2, pair, 0)


def turn_kernel(half, place, run, target, lh, ll, *refs):
    below = refs[: len(refs) - 8]
    vh, vl, bh, bl, ph, plo, th, tl = refs[len(refs) - 8 :]
    m = run.shape[0]
    for ti in pieces(m, 128):
        bh[ti, :], bl[ti, :] = split(run[ti, :])
        for tj in pieces(m, 128):
            th[ti, tj], tl[ti, tj] = split(target[tj, ti].T)
    for cs, value in multiply(th, tl, bh, bl):
        vh[:, cs], vl[:, cs] = split(value)
    first = True if not below else place[1] < half

    @pl.when(first)
    def _():
        for rs in pieces(m, 64):
            ph[rs, :], plo[rs, :] = lh[rs, :], ll[rs, :]

    if below:

        @pl.when(place[1] >= half)
        def _():
            for cs, value in multiply(lh, ll, *below):
                ph[:, cs], plo[:, cs] = split(value)


def final_kernel(
    count, place, picks, got, turned_h, turned_l, run_h, run_l, local_h, local_l, th, tl, table, out,
    gh, gl, ph, plo, vh, vl, x32, kh, kl, uh, ul,
):
    m = got.shape[0]
    coarse = place[0]
    for rs in pieces(m, 32):
        gh[rs, :], gl[rs, :] = split(got[rs, :])

    @pl.when(coarse == 0)
    def _():
        for rs in pieces(m, 64):
            ph[rs, :], plo[rs, :] = local_h[rs, :], local_l[rs, :]
        for cs in pieces(m, 256):
            vh[:, cs], vl[:, cs] = split(dot3(th, tl, gh, gl, cs))
        for cs in pieces(m, 256):
            x32[:, cs] = dot3(vh, vl, run_h, run_l, cs)

    @pl.when(coarse != 0)
    def _():
        for cs in pieces(m, 256):
            x32[:, cs] = dot3(turned_h, turned_l, gh, gl, cs)
        for cs in pieces(m, 256):
            ph[:, cs], plo[:, cs] = split(dot3(local_h, local_l, gh, gl, cs))

    for i, ti in enumerate(pieces(m, 128)):
        for tj in pieces(m, 128)[: i + 1]:
            value = 0.5 * (x32[tj, ti].T - x32[ti, tj])
            kh[ti, tj], kl[ti, tj] = split(value)
            if ti != tj:
                kh[tj, ti], kl[tj, ti] = split(-value.T)
    for cs in pieces(m, 256):
        uh[:, cs], ul[:, cs] = split(dot3(ph, plo, kh, kl, cs))
    totals = [jnp.zeros((8, 128), f32)] * count
    for cs in pieces(m, 256):
        for rs in pieces(m, 256):
            if rs.start < cs.start:
                continue
            value = (
                dot_nt(uh[rs, :], ph[cs, :]) + dot_nt(uh[rs, :], plo[cs, :]) + dot_nt(ul[rs, :], ph[cs, :])
            )
            for ti, tj in lower_tiles(m):
                if not (rs.start <= ti.start < rs.stop and cs.start <= tj.start < cs.stop):
                    continue
                tile = value[ti.start - rs.start : ti.stop - rs.start, tj.start - cs.start : tj.stop - cs.start]
                if ti != tj:
                    tile = tile + tile
                for c in range(count):
                    part = table[picks[0, c], ti, tj] * tile
                    for at in range(0, part.shape[0], 8):
                        totals[c] = totals[c] + part[at : at + 8, :]
    for c in range(count):
        out[0, c] = jnp.sum(totals[c])


def on_device(amplitudes, control_index, controls, drift_term, target):
    m = target.shape[0]
    kinds, count = controls.shape[0], amplitudes.shape[1]
    order = lax.axis_size("fine")
    assert amplitudes.shape[0] == 1 and lax.axis_size("coarse") == 2
    assert order & (order - 1) == 0 and order >= 4
    place = jnp.stack([lax.axis_index("coarse"), lax.axis_index("fine")]).astype(jnp.int32)
    square, half = pltpu.VMEM((m, m), f32), pltpu.VMEM((m, m), bf16)
    full = pltpu.VMEM((m, m), f32)
    short = order <= 8

    def params(mib):
        return pltpu.CompilerParams(vmem_limit_bytes=mib << 20)

    def cost(products):
        return pl.CostEstimate(
            flops=6 * products * m**3, bytes_accessed=12 * products * m * m, transcendentals=0
        )

    rows = fresh = (amplitudes, control_index)
    early = ()
    bit = 1
    while bit < order:
        coming = lax.ppermute(rows, "fine", [(i, i ^ bit) for i in range(order)])
        if bit == 1:
            table = pl.pallas_call(
                load_kernel,
                out_shape=pltpu.VMEM((kinds + 1, m, m), f32),
                in_specs=[HBM, HBM],
                out_specs=VMEM,
                scratch_shapes=[pltpu.SemaphoreType.DMA((kinds + 1,))],
                compiler_params=params(LOAD_MIB),
                cost_estimate=cost(2),
                name="load",
            )(outside(controls), outside(drift_term))
        elif short:
            width = fresh[0].shape[0]
            early = pl.pallas_call(
                functools.partial(build_kernel, bit - width),
                out_shape=(pltpu.VMEM((order // 2, m, m), bf16),) * 2,
                in_specs=[SMEM, SMEM] + [VMEM] * (1 + len(early)),
                out_specs=(VMEM, VMEM),
                scratch_shapes=Work.shapes(m) * width,
                input_output_aliases={3: 0, 4: 1} if early else {},
                compiler_params=params(BUILD_MIB),
                cost_estimate=cost(4 * width),
                name="build",
            )(*fresh, inside(table), *map(inside, early))
        rows = tuple(jnp.concatenate(pair, axis=0) for pair in zip(rows, coming))
        fresh = rows if bit == 1 else coming
        bit *= 2

    if short:
        kernel, taken = chain_kernel, (table, *early)
        outs = (square,) + (half,) * 4
        halves = [pltpu.VMEM((order // 2, m, m), bf16)] * 2
        scratch = halves * 2 + [pltpu.VMEM((2, m, m), bf16)] * 4 + Work.shapes(m) * (order // 2)
    else:
        kernel, taken, fresh = functools.partial(long_kernel, order), (table,), rows
        outs = (square, half, half)
        scratch = [pltpu.VMEM((2, m, m), bf16)] * 2 + [half] * 2 + Work.shapes(m) * 2
    run, *products = pl.pallas_call(
        kernel,
        out_shape=outs,
        in_specs=[SMEM] * 3 + [VMEM] * len(taken),
        out_specs=(VMEM,) * len(outs),
        scratch_shapes=scratch,
        compiler_params=params(CHAIN_MIB),
        cost_estimate=cost(23),
        name="chain",
    )(place, *fresh, *map(inside, taken))
    got = lax.ppermute(run, "coarse", [(0, 1), (1, 0)])
    turned = pl.pallas_call(
        functools.partial(turn_kernel, order // 2),
        out_shape=(half,) * 8,
        in_specs=[SMEM] + [VMEM] * (2 + len(products)),
        out_specs=(VMEM,) * 8,
        compiler_params=params(TURN_MIB),
        cost_estimate=cost(2),
        name="turn",
    )(place, inside(run), target, *map(inside, products))
    return pl.pallas_call(
        functools.partial(final_kernel, count),
        out_shape=jax.ShapeDtypeStruct((1, count), f32),
        in_specs=[SMEM, SMEM] + [VMEM] * 10,
        out_specs=SMEM,
        scratch_shapes=[half] * 6 + [full] + [half] * 4,
        compiler_params=params(FINAL_MIB),
        name="final",
    )(place, control_index, got, *map(inside, (*turned, table)))


LOAD_MIB = 4
BUILD_MIB = 14
CHAIN_MIB = 36
TURN_MIB = 6
FINAL_MIB = 12


def solution(mesh):
    placed = (
        P(("groups", "coarse", "fine"), None),
        P(("groups", "coarse", "fine"), None),
        P(),
        P(),
        P("groups", None),
    )
    return jax.shard_map(
        on_device,
        mesh=mesh,
        in_specs=placed,
        out_specs=P(("groups", "coarse", "fine"), None),
        check_vma=False,
    )
```

```python
import functools

import jax
import jax.numpy as jnp
from jax import lax
from jax.experimental import pallas as pl
from jax.experimental.pallas import tpu as pltpu
from jax.sharding import PartitionSpec as P

step_scale = 0.3
f32 = jnp.float32
bf16 = jnp.bfloat16
SMEM = pl.BlockSpec(memory_space=pltpu.SMEM)
VMEM = pl.BlockSpec(memory_space=pltpu.VMEM)
HBM = pl.BlockSpec(memory_space=pltpu.HBM)


def split(x):
    high = x.astype(bf16)
    return high, (x - high.astype(f32)).astype(bf16)


def dot(a, b):
    return jnp.dot(a, b, preferred_element_type=f32)


def dot_nt(a, b):
    return lax.dot_general(a, b, (((1,), (1,)), ((), ())), preferred_element_type=f32)


def pieces(m, size):
    size = size if m % size == 0 else m
    return [slice(at, at + size) for at in range(0, m, size)]


def dot3(ah, al, bh, bl, cols, rows=slice(None)):
    return (
        dot(ah[rows, :], bh[:, cols])
        + dot(ah[rows, :], bl[:, cols])
        + dot(al[rows, :], bh[:, cols])
    )


def lower_tiles(m):
    return [(ti, tj) for i, ti in enumerate(pieces(m, 128)) for tj in pieces(m, 128)[: i + 1]]


def skewed(ref):
    for ti, tj in lower_tiles(ref.shape[0]):
        ref[ti, tj] = (step_scale * 0.5) * (ref[ti, tj] - ref[tj, ti].T)


def generator(amps, picks, table, s):
    kinds = table.shape[0] - 1
    for ti, tj in lower_tiles(table.shape[1]):
        value = table[kinds, ti, tj]
        for amp, pick in zip(amps, picks):
            value = value + amp * table[pick, ti, tj]
        s.a32[ti, tj] = value
        s.ah[ti, tj], s.al[ti, tj] = split(value)
        if ti != tj:
            back = -value.T
            s.a32[tj, ti] = back
            s.ah[tj, ti], s.al[tj, ti] = split(back)


def mirrored(ah, al, bh, bl, sign, put):
    m = ah.shape[0]
    for cs in pieces(m, 256):
        value = dot3(ah, al, bh, bl, cs, slice(cs.start, m))
        put(slice(cs.start, m), cs, value)
        width = cs.stop - cs.start
        for rs in pieces(m, 256):
            if rs.start > cs.start:
                at = rs.start - cs.start
                flipped = value[at : at + width, :].T
                put(cs, rs, flipped if sign > 0 else -flipped)


def square_step(s):
    def put(rows, cols, value):
        s.b32[rows, cols] = value
        s.bh[rows, cols], s.bl[rows, cols] = split(value)

    mirrored(s.ah, s.al, s.ah, s.al, 1, put)


def cube_step(s):
    def put(rows, cols, value):
        s.dh[rows, cols], s.dl[rows, cols] = split(value)
        a, b = s.a32[rows, cols], s.b32[rows, cols]
        rest = a * (1 / 24) + b * (1 / 120) + value * (1 / 720)
        s.qh[rows, cols], s.ql[rows, cols] = split(rest)
        s.a32[rows, cols] = a + b * 0.5 + value * (1 / 6)

    mirrored(s.ah, s.al, s.bh, s.bl, -1, put)


def last_step(s, wh, wl):
    m = s.ah.shape[0]
    for cs in pieces(m, 256):
        value = dot3(s.dh, s.dl, s.qh, s.ql, cs) + s.a32[:, cs]
        for rs in pieces(m, 256):
            part = value[rs, :]
            if rs == cs:
                part = part + unit(part.shape)
            wh[rs, cs], wl[rs, cs] = split(part)


def unit(shape):
    return (
        lax.broadcasted_iota(jnp.int32, shape, 0) == lax.broadcasted_iota(jnp.int32, shape, 1)
    ).astype(f32)


def inside(x):
    return pltpu.with_memory_space_constraint(x, pltpu.VMEM)


def outside(x):
    return pltpu.with_memory_space_constraint(x, pltpu.HBM)


class Work:
    names = ("a32", "b32", "ah", "al", "bh", "bl", "dh", "dl", "qh", "ql")

    def __init__(self, refs):
        for name, ref in zip(self.names, refs):
            setattr(self, name, ref)

    @classmethod
    def shapes(cls, m):
        return [pltpu.VMEM((m, m), f32)] * 2 + [pltpu.VMEM((m, m), bf16)] * 8


def propagators(amps, picks, picked, works, table, wh, wl, slots):
    count = amps.shape[1]
    for row, s in zip(picked, works):
        generator([amps[row, c] for c in range(count)], [picks[row, c] for c in range(count)], table, s)
    for s in works:
        square_step(s)
    for s in works:
        cube_step(s)
    for slot, s in zip(slots, works):
        last_step(s, wh.at[slot], wl.at[slot])


def load_kernel(controls, drift, table, sems):
    kinds = controls.shape[0]

    def copy(k):
        return pltpu.make_async_copy(controls.at[k], table.at[k], sems.at[k])

    last = pltpu.make_async_copy(drift, table.at[kinds], sems.at[kinds])
    copies = [copy(k) for k in range(kinds)] + [last]
    groups = [range(at, min(at + 3, kinds + 1)) for at in range(0, kinds + 1, 3)]
    for k in range(min(6, kinds + 1)):
        copies[k].start()
    for n, group in enumerate(groups):
        for k in group:
            copies[k].wait()
        for k in groups[n + 2] if n + 2 < len(groups) else ():
            copies[k].start()
        for k in group:
            skewed(table.at[k])


def works_of(scratch):
    size = len(Work.names)
    return [Work(scratch[at : at + size]) for at in range(0, len(scratch), size)]


def build_kernel(first, amps, picks, table, *refs):
    size = len(Work.names)
    width = amps.shape[0]
    wh, wl = refs[-2 - width * size : -width * size]
    slots = [first + n for n in range(width)]
    propagators(amps, picks, range(width), works_of(refs[-width * size :]), table, wh, wl, slots)


def multiply(ah, al, bh, bl):
    for cs in pieces(ah.shape[0], 256):
        yield cs, dot3(ah, al, bh, bl, cs)


def chain_kernel(
    place, amps, picks, table, early_h, early_l, run, lh, ll, oh, ol,
    wh, wl, th, tl, qh, ql, bh, bl, *scratch
):
    half, m = early_h.shape[:2]
    fine = place[1]
    inner = fine & (half - 1)
    upper = jnp.where(fine < half, 1, 0)
    propagators(amps, picks, range(half), works_of(scratch), table, wh, wl, range(half))
    for rs in pieces(m, 64):
        high, low = early_h[inner, rs, :], early_l[inner, rs, :]
        qh[0, rs, :], ql[0, rs, :] = high, low
        bh[0, rs, :], bl[0, rs, :] = high, low
    for step in range(1, half):
        slot = step ^ inner
        side = jnp.where(step <= inner, 0, 1)
        for cs, value in multiply(early_h.at[slot], early_l.at[slot], qh.at[0], ql.at[0]):
            high, low = split(value)
            qh[0, :, cs], ql[0, :, cs] = high, low
            bh[side, :, cs], bl[side, :, cs] = high, low
    for rs in pieces(m, 64):
        lh[rs, :], ll[rs, :] = bh[0, rs, :], bl[0, rs, :]
    level = [(wh.at[step ^ inner], wl.at[step ^ inner]) for step in range(half)]
    free = 0
    while len(level) > 1:
        above = []
        for n in range(0, len(level), 2):
            goal = (qh.at[1], ql.at[1]) if len(level) == 2 else (th.at[free], tl.at[free])
            free += 1
            for cs, value in multiply(*level[n + 1], *level[n]):
                goal[0][:, cs], goal[1][:, cs] = split(value)
            above.append(goal)
        level = above
    for cs, value in multiply(qh.at[upper], ql.at[upper], qh.at[1 - upper], ql.at[1 - upper]):
        run[:, cs] = value
    for rs in pieces(m, 64):
        oh[rs, :], ol[rs, :] = qh[1, rs, :], ql[1, rs, :]


def long_kernel(order, place, amps, picks, table, run, lh, ll, wh, wl, rh, rl, *scratch):
    works = works_of(scratch)
    m = run.shape[0]
    fine = place[1]
    for rs in pieces(m, 256):
        for cs in pieces(m, 256):
            shape = (rs.stop - rs.start, cs.stop - cs.start)
            rh[rs, cs], rl[rs, cs] = split(unit(shape) if rs == cs else jnp.zeros(shape, f32))

    def pair(n, carry):
        steps = [2 * n, 2 * n + 1]
        propagators(amps, picks, [step ^ fine for step in steps], works, table, wh, wl, range(2))
        for k, step in enumerate(steps):
            for cs, value in multiply(wh.at[k], wl.at[k], rh, rl):
                run[:, cs] = value
                rh[:, cs], rl[:, cs] = split(value)

            @pl.when(step == fine)
            def _():
                for rs in pieces(m, 64):
                    lh[rs, :], ll[rs, :] = rh[rs, :], rl[rs, :]

        return carry

    lax.fori_loop(0, order // 2, pair, 0)


def multiply_nt(ah, al, bh, bl, rows=slice(None)):
    for cs in pieces(bh.shape[0], 256):
        yield cs, (
            dot_nt(ah[rows, :], bh[cs, :]) + dot_nt(ah[rows, :], bl[cs, :]) + dot_nt(al[rows, :], bh[cs, :])
        )


def turn_kernel(half, place, run, target, lh, ll, *refs):
    below = refs[: len(refs) - 10]
    eh, el, fh, fl, bh, bl, th, tl, ph, plo = refs[len(refs) - 10 :]
    m = run.shape[0]
    for rs in pieces(m, 32):
        bh[rs, :], bl[rs, :] = split(run[rs, :])
    later = place[1] >= half if below else False

    @pl.when(jnp.logical_not(later))
    def _():
        for rs in pieces(m, 64):
            ph[rs, :], plo[rs, :] = lh[rs, :], ll[rs, :]

    if below:

        @pl.when(later)
        def _():
            for cs, value in multiply(lh, ll, *below):
                ph[:, cs], plo[:, cs] = split(value)

    @pl.when(place[0] == 0)
    def _():
        for rs in pieces(m, 32):
            th[rs, :], tl[rs, :] = split(target[rs, :])
        for cs, value in multiply_nt(ph, plo, bh, bl):
            eh[:, cs], el[:, cs] = split(value)
        for cs, value in multiply_nt(ph, plo, th, tl):
            fh[:, cs], fl[:, cs] = split(value)

    @pl.when(place[0] != 0)
    def _():
        for ti in pieces(m, 128):
            for tj in pieces(m, 128):
                th[ti, tj], tl[ti, tj] = split(target[tj, ti].T)
        for cs, value in multiply(th, tl, bh, bl):
            eh[:, cs], el[:, cs] = split(value)
        for rs in pieces(m, 64):
            fh[rs, :], fl[rs, :] = ph[rs, :], plo[rs, :]


def final_kernel(place, picks, got, eh, el, fh, fl, table, out, gh, gl, x32, ph, plo, kh, kl, uh, ul):
    m = got.shape[0]
    count = picks.shape[1]

    def put(tiles_of):
        totals = [jnp.zeros((8, min(m, 128)), f32)] * count
        for ti, tj, tile in tiles_of:
            for c in range(count):
                part = table[picks[0, c], ti, tj] * tile
                for at in range(0, part.shape[0], 8):
                    totals[c] = totals[c] + part[at : at + 8, :]
        for c in range(count):
            out[0, c] = jnp.sum(totals[c])

    for rs in pieces(m, 32):
        gh[rs, :], gl[rs, :] = split(got[rs, :])

    @pl.when(place[0] == 0)
    def _():
        for cs, value in multiply(fh, fl, gh, gl):
            kh[:, cs], kl[:, cs] = split(value)
        for cs, value in multiply_nt(eh, el, kh, kl):
            x32[:, cs] = value

        def tiles_of():
            for ti, tj in lower_tiles(m):
                yield ti, tj, x32[ti, tj] if ti == tj else x32[ti, tj] - x32[tj, ti].T

        put(tiles_of())

    @pl.when(place[0] != 0)
    def _():
        for cs, value in multiply(eh, el, gh, gl):
            x32[:, cs] = value
        for cs, value in multiply(fh, fl, gh, gl):
            ph[:, cs], plo[:, cs] = split(value)
        for ti, tj in lower_tiles(m):
            value = 0.5 * (x32[tj, ti].T - x32[ti, tj])
            kh[ti, tj], kl[ti, tj] = split(value)
            if ti != tj:
                kh[tj, ti], kl[tj, ti] = split(-value.T)
        for cs, value in multiply(ph, plo, kh, kl):
            uh[:, cs], ul[:, cs] = split(value)

        def tiles_of():
            for rs in pieces(m, 256):
                for cs, value in multiply_nt(uh, ul, ph.at[: rs.stop], plo.at[: rs.stop], rs):
                    for ti, tj in lower_tiles(m):
                        if rs.start <= ti.start < rs.stop and cs.start <= tj.start < cs.stop:
                            tile = value[
                                ti.start - rs.start : ti.stop - rs.start, tj.start - cs.start : tj.stop - cs.start
                            ]
                            yield ti, tj, tile if ti == tj else tile + tile

        put(tiles_of())


def on_device(amplitudes, control_index, controls, drift_term, target):
    m = target.shape[0]
    kinds, count = controls.shape[0], amplitudes.shape[1]
    order = lax.axis_size("fine")
    assert amplitudes.shape[0] == 1 and lax.axis_size("coarse") == 2
    assert order & (order - 1) == 0 and order >= 4
    place = jnp.stack([lax.axis_index("coarse"), lax.axis_index("fine")]).astype(jnp.int32)
    square, half = pltpu.VMEM((m, m), f32), pltpu.VMEM((m, m), bf16)
    full = pltpu.VMEM((m, m), f32)
    short = order <= 8

    def params(mib):
        return pltpu.CompilerParams(vmem_limit_bytes=mib << 20)

    def cost(products):
        return pl.CostEstimate(
            flops=6 * products * m**3, bytes_accessed=12 * products * m * m, transcendentals=0
        )

    rows = fresh = (amplitudes, control_index)
    early = ()
    bit = 1
    while bit < order:
        coming = lax.ppermute(rows, "fine", [(i, i ^ bit) for i in range(order)])
        if bit == 1:
            table = pl.pallas_call(
                load_kernel,
                out_shape=pltpu.VMEM((kinds + 1, m, m), f32),
                in_specs=[HBM, HBM],
                out_specs=VMEM,
                scratch_shapes=[pltpu.SemaphoreType.DMA((kinds + 1,))],
                compiler_params=params(LOAD_MIB),
                cost_estimate=cost(2),
                name="load",
            )(outside(controls), outside(drift_term))
        elif short:
            width = fresh[0].shape[0]
            early = pl.pallas_call(
                functools.partial(build_kernel, bit - width),
                out_shape=(pltpu.VMEM((order // 2, m, m), bf16),) * 2,
                in_specs=[SMEM, SMEM] + [VMEM] * (1 + len(early)),
                out_specs=(VMEM, VMEM),
                scratch_shapes=Work.shapes(m) * width,
                input_output_aliases={3: 0, 4: 1} if early else {},
                compiler_params=params(BUILD_MIB),
                cost_estimate=cost(4 * width),
                name="build",
            )(*fresh, inside(table), *map(inside, early))
        rows = tuple(jnp.concatenate(pair, axis=0) for pair in zip(rows, coming))
        fresh = rows if bit == 1 else coming
        bit *= 2

    if short:
        kernel, taken = chain_kernel, (table, *early)
        outs = (square,) + (half,) * 4
        halves = [pltpu.VMEM((order // 2, m, m), bf16)] * 2
        scratch = halves * 2 + [pltpu.VMEM((2, m, m), bf16)] * 4 + Work.shapes(m) * (order // 2)
    else:
        kernel, taken, fresh = functools.partial(long_kernel, order), (table,), rows
        outs = (square, half, half)
        scratch = [pltpu.VMEM((2, m, m), bf16)] * 2 + [half] * 2 + Work.shapes(m) * 2
    run, *products = pl.pallas_call(
        kernel,
        out_shape=outs,
        in_specs=[SMEM] * 3 + [VMEM] * len(taken),
        out_specs=(VMEM,) * len(outs),
        scratch_shapes=scratch,
        compiler_params=params(CHAIN_MIB),
        cost_estimate=cost(23),
        name="chain",
    )(place, *fresh, *map(inside, taken))
    got = lax.ppermute(run, "coarse", [(0, 1), (1, 0)])
    turned = pl.pallas_call(
        functools.partial(turn_kernel, order // 2),
        out_shape=(half,) * 4,
        in_specs=[SMEM] + [VMEM] * (2 + len(products)),
        out_specs=(VMEM,) * 4,
        scratch_shapes=[half] * 6,
        compiler_params=params(TURN_MIB),
        cost_estimate=cost(2),
        name="turn",
    )(place, inside(run), target, *map(inside, products))
    return pl.pallas_call(
        final_kernel,
        out_shape=jax.ShapeDtypeStruct((1, count), f32),
        in_specs=[SMEM, SMEM] + [VMEM] * 6,
        out_specs=SMEM,
        scratch_shapes=[half] * 2 + [full] + [half] * 6,
        compiler_params=params(FINAL_MIB),
        name="final",
    )(place, control_index, got, *map(inside, (*turned, table)))


LOAD_MIB = 4
BUILD_MIB = 14
CHAIN_MIB = 36
TURN_MIB = 6
FINAL_MIB = 12


def solution(mesh):
    placed = (
        P(("groups", "coarse", "fine"), None),
        P(("groups", "coarse", "fine"), None),
        P(),
        P(),
        P("groups", None),
    )
    return jax.shard_map(
        on_device,
        mesh=mesh,
        in_specs=placed,
        out_specs=P(("groups", "coarse", "fine"), None),
        check_vma=False,
    )
```

```python
import functools

import jax
import jax.numpy as jnp
from jax import lax
from jax.experimental import pallas as pl
from jax.experimental.pallas import tpu as pltpu
from jax.sharding import PartitionSpec as P

step_scale = 0.3
f32 = jnp.float32
bf16 = jnp.bfloat16
SMEM = pl.BlockSpec(memory_space=pltpu.SMEM)
VMEM = pl.BlockSpec(memory_space=pltpu.VMEM)
HBM = pl.BlockSpec(memory_space=pltpu.HBM)


def split(x):
    high = x.astype(bf16)
    return high, (x - high.astype(f32)).astype(bf16)


def dot(a, b):
    return jnp.dot(a, b, preferred_element_type=f32)


def dot_nt(a, b):
    return lax.dot_general(a, b, (((1,), (1,)), ((), ())), preferred_element_type=f32)


def pieces(m, size):
    size = size if m % size == 0 else m
    return [slice(at, at + size) for at in range(0, m, size)]


def dot3(ah, al, bh, bl, cols, rows=slice(None)):
    return (
        dot(ah[rows, :], bh[:, cols])
        + dot(ah[rows, :], bl[:, cols])
        + dot(al[rows, :], bh[:, cols])
    )


def lower_tiles(m):
    return [(ti, tj) for i, ti in enumerate(pieces(m, 128)) for tj in pieces(m, 128)[: i + 1]]


def skewed(ref):
    for ti, tj in lower_tiles(ref.shape[0]):
        ref[ti, tj] = (step_scale * 0.5) * (ref[ti, tj] - ref[tj, ti].T)


def generator(amps, picks, table, s):
    kinds = table.shape[0] - 1
    for ti, tj in lower_tiles(table.shape[1]):
        value = table[kinds, ti, tj]
        for amp, pick in zip(amps, picks):
            value = value + amp * table[pick, ti, tj]
        s.a32[ti, tj] = value
        s.ah[ti, tj], s.al[ti, tj] = split(value)
        if ti != tj:
            back = -value.T
            s.a32[tj, ti] = back
            s.ah[tj, ti], s.al[tj, ti] = split(back)


def mirrored(ah, al, bh, bl, sign, put):
    m = ah.shape[0]
    for cs in pieces(m, 256):
        value = dot3(ah, al, bh, bl, cs, slice(cs.start, m))
        put(slice(cs.start, m), cs, value)
        width = cs.stop - cs.start
        for rs in pieces(m, 256):
            if rs.start > cs.start:
                at = rs.start - cs.start
                flipped = value[at : at + width, :].T
                put(cs, rs, flipped if sign > 0 else -flipped)


def square_step(s):
    def put(rows, cols, value):
        s.b32[rows, cols] = value
        s.bh[rows, cols], s.bl[rows, cols] = split(value)

    mirrored(s.ah, s.al, s.ah, s.al, 1, put)


def cube_step(s):
    def put(rows, cols, value):
        s.dh[rows, cols], s.dl[rows, cols] = split(value)
        a, b = s.a32[rows, cols], s.b32[rows, cols]
        rest = a * (1 / 24) + b * (1 / 120) + value * (1 / 720)
        s.qh[rows, cols], s.ql[rows, cols] = split(rest)
        s.a32[rows, cols] = a + b * 0.5 + value * (1 / 6)

    mirrored(s.ah, s.al, s.bh, s.bl, -1, put)


def last_step(s, wh, wl):
    m = s.ah.shape[0]
    for cs in pieces(m, 256):
        value = dot3(s.dh, s.dl, s.qh, s.ql, cs) + s.a32[:, cs]
        for rs in pieces(m, 256):
            part = value[rs, :]
            if rs == cs:
                part = part + unit(part.shape)
            wh[rs, cs], wl[rs, cs] = split(part)


def unit(shape):
    return (
        lax.broadcasted_iota(jnp.int32, shape, 0) == lax.broadcasted_iota(jnp.int32, shape, 1)
    ).astype(f32)


def inside(x):
    return pltpu.with_memory_space_constraint(x, pltpu.VMEM)


def outside(x):
    return pltpu.with_memory_space_constraint(x, pltpu.HBM)


class Work:
    names = ("a32", "b32", "ah", "al", "bh", "bl", "dh", "dl", "qh", "ql")

    def __init__(self, refs):
        for name, ref in zip(self.names, refs):
            setattr(self, name, ref)

    @classmethod
    def shapes(cls, m):
        return [pltpu.VMEM((m, m), f32)] * 2 + [pltpu.VMEM((m, m), bf16)] * 8


def propagators(rows, picked, works, table, wh, wl, slots):
    count = rows.shape[1] // 2
    for row, s in zip(picked, works):
        amps = [rows[row, c] for c in range(count)]
        picks = [rows[row, count + c].astype(jnp.int32) for c in range(count)]
        generator(amps, picks, table, s)
    for s in works:
        square_step(s)
    for s in works:
        cube_step(s)
    for slot, s in zip(slots, works):
        last_step(s, wh.at[slot], wl.at[slot])


def load_kernel(controls, drift, table, sems):
    kinds = controls.shape[0]

    def copy(k):
        return pltpu.make_async_copy(controls.at[k], table.at[k], sems.at[k])

    last = pltpu.make_async_copy(drift, table.at[kinds], sems.at[kinds])
    copies = [copy(k) for k in range(kinds)] + [last]
    for each in copies:
        each.start()
    for at in range(0, kinds + 1, 3):
        group = range(at, min(at + 3, kinds + 1))
        for k in group:
            copies[k].wait()
        for k in group:
            skewed(table.at[k])


def works_of(scratch):
    size = len(Work.names)
    return [Work(scratch[at : at + size]) for at in range(0, len(scratch), size)]


def build_kernel(first, rows, table, *refs):
    size = len(Work.names)
    width = rows.shape[0]
    wh, wl = refs[-2 - width * size : -width * size]
    slots = [first + n for n in range(width)]
    propagators(rows, range(width), works_of(refs[-width * size :]), table, wh, wl, slots)


def multiply(ah, al, bh, bl):
    for cs in pieces(ah.shape[0], 256):
        yield cs, dot3(ah, al, bh, bl, cs)


def chain_kernel(
    place, rows, table, early_h, early_l, run, lh, ll, oh, ol,
    wh, wl, th, tl, qh, ql, bh, bl, *scratch
):
    half, m = early_h.shape[:2]
    fine = place[1]
    inner = fine & (half - 1)
    upper = jnp.where(fine < half, 1, 0)
    propagators(rows, range(half), works_of(scratch), table, wh, wl, range(half))
    for rs in pieces(m, 64):
        high, low = early_h[inner, rs, :], early_l[inner, rs, :]
        qh[0, rs, :], ql[0, rs, :] = high, low
        bh[0, rs, :], bl[0, rs, :] = high, low
    for step in range(1, half):
        slot = step ^ inner
        side = jnp.where(step <= inner, 0, 1)
        for cs, value in multiply(early_h.at[slot], early_l.at[slot], qh.at[0], ql.at[0]):
            high, low = split(value)
            qh[0, :, cs], ql[0, :, cs] = high, low
            bh[side, :, cs], bl[side, :, cs] = high, low
    for rs in pieces(m, 64):
        lh[rs, :], ll[rs, :] = bh[0, rs, :], bl[0, rs, :]
    level = [(wh.at[step ^ inner], wl.at[step ^ inner]) for step in range(half)]
    free = 0
    while len(level) > 1:
        above = []
        for n in range(0, len(level), 2):
            goal = (qh.at[1], ql.at[1]) if len(level) == 2 else (th.at[free], tl.at[free])
            free += 1
            for cs, value in multiply(*level[n + 1], *level[n]):
                goal[0][:, cs], goal[1][:, cs] = split(value)
            above.append(goal)
        level = above
    for cs, value in multiply(qh.at[upper], ql.at[upper], qh.at[1 - upper], ql.at[1 - upper]):
        run[:, cs] = value
    for rs in pieces(m, 64):
        oh[rs, :], ol[rs, :] = qh[1, rs, :], ql[1, rs, :]

    @pl.when((place[0] != 0) & (fine >= half))
    def _():
        for cs, value in multiply(bh.at[0], bl.at[0], qh.at[1], ql.at[1]):
            lh[:, cs], ll[:, cs] = split(value)


def long_kernel(order, place, rows, table, run, lh, ll, wh, wl, rh, rl, *scratch):
    works = works_of(scratch)
    m = run.shape[0]
    fine = place[1]
    for rs in pieces(m, 256):
        for cs in pieces(m, 256):
            shape = (rs.stop - rs.start, cs.stop - cs.start)
            rh[rs, cs], rl[rs, cs] = split(unit(shape) if rs == cs else jnp.zeros(shape, f32))

    def pair(n, carry):
        steps = [2 * n, 2 * n + 1]
        propagators(rows, [step ^ fine for step in steps], works, table, wh, wl, range(2))
        for k, step in enumerate(steps):
            for cs, value in multiply(wh.at[k], wl.at[k], rh, rl):
                run[:, cs] = value
                rh[:, cs], rl[:, cs] = split(value)

            @pl.when(step == fine)
            def _():
                for rs in pieces(m, 64):
                    lh[rs, :], ll[rs, :] = rh[rs, :], rl[rs, :]

        return carry

    lax.fori_loop(0, order // 2, pair, 0)


def multiply_nt(ah, al, bh, bl, rows=slice(None)):
    for cs in pieces(bh.shape[0], 256):
        yield cs, (
            dot_nt(ah[rows, :], bh[cs, :]) + dot_nt(ah[rows, :], bl[cs, :]) + dot_nt(al[rows, :], bh[cs, :])
        )


def turn_kernel(half, place, run, target, lh, ll, *refs):
    below = refs[: len(refs) - 10]
    eh, el, fh, fl, bh, bl, th, tl, ph, plo = refs[len(refs) - 10 :]
    m = run.shape[0]
    for rs in pieces(m, 32):
        bh[rs, :], bl[rs, :] = split(run[rs, :])
    later = (place[0] == 0) & (place[1] >= half) if below else False

    @pl.when(jnp.logical_not(later))
    def _():
        for rs in pieces(m, 64):
            ph[rs, :], plo[rs, :] = lh[rs, :], ll[rs, :]

    if below:

        @pl.when(later)
        def _():
            for cs, value in multiply(lh, ll, *below):
                ph[:, cs], plo[:, cs] = split(value)

    @pl.when(place[0] == 0)
    def _():
        for rs in pieces(m, 32):
            th[rs, :], tl[rs, :] = split(target[rs, :])
        for cs, value in multiply_nt(ph, plo, bh, bl):
            eh[:, cs], el[:, cs] = split(value)
        for cs, value in multiply_nt(ph, plo, th, tl):
            fh[:, cs], fl[:, cs] = split(value)

    @pl.when(place[0] != 0)
    def _():
        for ti in pieces(m, 128):
            for tj in pieces(m, 128):
                th[ti, tj], tl[ti, tj] = split(target[tj, ti].T)
        for cs, value in multiply(th, tl, bh, bl):
            eh[:, cs], el[:, cs] = split(value)
        for rs in pieces(m, 64):
            fh[rs, :], fl[rs, :] = ph[rs, :], plo[rs, :]


def final_kernel(place, picks, got, eh, el, fh, fl, table, out, gh, gl, x32, ph, plo, kh, kl, uh, ul):
    m = got.shape[0]
    count = picks.shape[1]

    def put(tiles_of):
        totals = [jnp.zeros((8, min(m, 128)), f32)] * count
        for ti, tj, tile in tiles_of:
            for c in range(count):
                part = table[picks[0, c], ti, tj] * tile
                for at in range(0, part.shape[0], 8):
                    totals[c] = totals[c] + part[at : at + 8, :]
        for c in range(count):
            out[0, c] = jnp.sum(totals[c])

    for rs in pieces(m, 32):
        gh[rs, :], gl[rs, :] = split(got[rs, :])

    @pl.when(place[0] == 0)
    def _():
        for cs, value in multiply(fh, fl, gh, gl):
            kh[:, cs], kl[:, cs] = split(value)
        for cs, value in multiply_nt(eh, el, kh, kl):
            x32[:, cs] = value

        def tiles_of():
            for ti, tj in lower_tiles(m):
                yield ti, tj, x32[ti, tj] if ti == tj else x32[ti, tj] - x32[tj, ti].T

        put(tiles_of())

    @pl.when(place[0] != 0)
    def _():
        for cs, value in multiply(eh, el, gh, gl):
            x32[:, cs] = value
        for cs, value in multiply(fh, fl, gh, gl):
            ph[:, cs], plo[:, cs] = split(value)
        for ti, tj in lower_tiles(m):
            value = 0.5 * (x32[tj, ti].T - x32[ti, tj])
            kh[ti, tj], kl[ti, tj] = split(value)
            if ti != tj:
                kh[tj, ti], kl[tj, ti] = split(-value.T)
        for cs, value in multiply(ph, plo, kh, kl):
            uh[:, cs], ul[:, cs] = split(value)

        def tiles_of():
            for rs in pieces(m, 256):
                for cs, value in multiply_nt(uh, ul, ph.at[: rs.stop], plo.at[: rs.stop], rs):
                    for ti, tj in lower_tiles(m):
                        if rs.start <= ti.start < rs.stop and cs.start <= tj.start < cs.stop:
                            tile = value[
                                ti.start - rs.start : ti.stop - rs.start, tj.start - cs.start : tj.stop - cs.start
                            ]
                            yield ti, tj, tile if ti == tj else tile + tile

        put(tiles_of())


def on_device(amplitudes, control_index, controls, drift_term, target):
    m = target.shape[0]
    kinds, count = controls.shape[0], amplitudes.shape[1]
    order = lax.axis_size("fine")
    assert amplitudes.shape[0] == 1 and lax.axis_size("coarse") == 2
    assert order & (order - 1) == 0 and order >= 4
    place = jnp.stack([lax.axis_index("coarse"), lax.axis_index("fine")]).astype(jnp.int32)
    square, half = pltpu.VMEM((m, m), f32), pltpu.VMEM((m, m), bf16)
    full = pltpu.VMEM((m, m), f32)
    short = order <= 8

    def params(mib):
        return pltpu.CompilerParams(vmem_limit_bytes=mib << 20)

    def cost(products):
        return pl.CostEstimate(
            flops=6 * products * m**3, bytes_accessed=12 * products * m * m, transcendentals=0
        )

    rows = fresh = coming = None
    early = ()
    bit = 1
    while bit < order:
        swap = [(i, i ^ bit) for i in range(order)]
        if bit == 1:
            pairs = (amplitudes, control_index), lax.ppermute((amplitudes, control_index), "fine", swap)
        else:
            coming = lax.ppermute(rows, "fine", swap)
        if bit == 1:
            table = pl.pallas_call(
                load_kernel,
                out_shape=pltpu.VMEM((kinds + 1, m, m), f32),
                in_specs=[HBM, HBM],
                out_specs=VMEM,
                scratch_shapes=[pltpu.SemaphoreType.DMA((kinds + 1,))],
                compiler_params=params(LOAD_MIB),
                cost_estimate=cost(2),
                name="load",
            )(outside(controls), outside(drift_term))
        elif short:
            width = fresh.shape[0]
            early = pl.pallas_call(
                functools.partial(build_kernel, bit - width),
                out_shape=(pltpu.VMEM((order // 2, m, m), bf16),) * 2,
                in_specs=[SMEM] + [VMEM] * (1 + len(early)),
                out_specs=(VMEM, VMEM),
                scratch_shapes=Work.shapes(m) * width,
                input_output_aliases={2: 0, 3: 1} if early else {},
                compiler_params=params(BUILD_MIB),
                cost_estimate=cost(4 * width),
                name="build",
            )(fresh, inside(table), *map(inside, early))
        if bit == 1:
            amps, picks = lax.optimization_barrier([jnp.concatenate(each, axis=0) for each in zip(*pairs)])
            rows = fresh = jnp.concatenate([amps, picks.astype(f32)], axis=1)
        else:
            rows, fresh = jnp.concatenate([rows, coming], axis=0), coming
        bit *= 2

    if short:
        kernel, taken = chain_kernel, (table, *early)
        outs = (square,) + (half,) * 4
        halves = [pltpu.VMEM((order // 2, m, m), bf16)] * 2
        scratch = halves * 2 + [pltpu.VMEM((2, m, m), bf16)] * 4 + Work.shapes(m) * (order // 2)
    else:
        kernel, taken, fresh = functools.partial(long_kernel, order), (table,), rows
        outs = (square, half, half)
        scratch = [pltpu.VMEM((2, m, m), bf16)] * 2 + [half] * 2 + Work.shapes(m) * 2
    run, *products = pl.pallas_call(
        kernel,
        out_shape=outs,
        in_specs=[SMEM] * 2 + [VMEM] * len(taken),
        out_specs=(VMEM,) * len(outs),
        scratch_shapes=scratch,
        compiler_params=params(CHAIN_MIB),
        cost_estimate=cost(23),
        name="chain",
    )(place, fresh, *map(inside, taken))
    got = lax.ppermute(run, "coarse", [(0, 1), (1, 0)])
    turned = pl.pallas_call(
        functools.partial(turn_kernel, order // 2),
        out_shape=(half,) * 4,
        in_specs=[SMEM] + [VMEM] * (2 + len(products)),
        out_specs=(VMEM,) * 4,
        scratch_shapes=[half] * 6,
        compiler_params=params(TURN_MIB),
        cost_estimate=cost(2),
        name="turn",
    )(place, inside(run), target, *map(inside, products))
    return pl.pallas_call(
        final_kernel,
        out_shape=jax.ShapeDtypeStruct((1, count), f32),
        in_specs=[SMEM, SMEM] + [VMEM] * 6,
        out_specs=SMEM,
        scratch_shapes=[half] * 2 + [full] + [half] * 6,
        compiler_params=params(FINAL_MIB),
        name="final",
    )(place, control_index, got, *map(inside, (*turned, table)))


LOAD_MIB = 4
BUILD_MIB = 14
CHAIN_MIB = 36
TURN_MIB = 6
FINAL_MIB = 12


def solution(mesh):
    placed = (
        P(("groups", "coarse", "fine"), None),
        P(("groups", "coarse", "fine"), None),
        P(),
        P(),
        P("groups", None),
    )
    return jax.shard_map(
        on_device,
        mesh=mesh,
        in_specs=placed,
        out_specs=P(("groups", "coarse", "fine"), None),
        check_vma=False,
    )
```

```python
import functools

import jax
import jax.numpy as jnp
from jax import lax
from jax.experimental import pallas as pl
from jax.experimental.pallas import tpu as pltpu
from jax.sharding import PartitionSpec as P

step_scale = 0.3
f32 = jnp.float32
bf16 = jnp.bfloat16
SMEM = pl.BlockSpec(memory_space=pltpu.SMEM)
VMEM = pl.BlockSpec(memory_space=pltpu.VMEM)
HBM = pl.BlockSpec(memory_space=pltpu.HBM)


def split(x):
    high = x.astype(bf16)
    return high, (x - high.astype(f32)).astype(bf16)


def dot(a, b):
    return jnp.dot(a, b, preferred_element_type=f32)


def dot_nt(a, b):
    return lax.dot_general(a, b, (((1,), (1,)), ((), ())), preferred_element_type=f32)


def pieces(m, size):
    size = size if m % size == 0 else m
    return [slice(at, at + size) for at in range(0, m, size)]


def dot3(ah, al, bh, bl, cols, rows=slice(None)):
    return (
        dot(ah[rows, :], bh[:, cols])
        + dot(ah[rows, :], bl[:, cols])
        + dot(al[rows, :], bh[:, cols])
    )


def lower_tiles(m):
    return [(ti, tj) for i, ti in enumerate(pieces(m, 128)) for tj in pieces(m, 128)[: i + 1]]


def skewed(ref):
    for ti, tj in lower_tiles(ref.shape[0]):
        ref[ti, tj] = (step_scale * 0.5) * (ref[ti, tj] - ref[tj, ti].T)


def generator(amps, picks, table, s):
    kinds = table.shape[0] - 1
    for ti, tj in lower_tiles(table.shape[1]):
        value = table[kinds, ti, tj]
        for amp, pick in zip(amps, picks):
            value = value + amp * table[pick, ti, tj]
        s.a32[ti, tj] = value
        s.ah[ti, tj], s.al[ti, tj] = split(value)
        if ti != tj:
            back = -value.T
            s.a32[tj, ti] = back
            s.ah[tj, ti], s.al[tj, ti] = split(back)


def mirrored(ah, al, bh, bl, sign, put):
    m = ah.shape[0]
    for cs in pieces(m, 256):
        value = dot3(ah, al, bh, bl, cs, slice(cs.start, m))
        put(slice(cs.start, m), cs, value)
        width = cs.stop - cs.start
        for rs in pieces(m, 256):
            if rs.start > cs.start:
                at = rs.start - cs.start
                flipped = value[at : at + width, :].T
                put(cs, rs, flipped if sign > 0 else -flipped)


def square_step(s):
    def put(rows, cols, value):
        s.b32[rows, cols] = value
        s.bh[rows, cols], s.bl[rows, cols] = split(value)

    mirrored(s.ah, s.al, s.ah, s.al, 1, put)


def cube_step(s):
    def put(rows, cols, value):
        s.dh[rows, cols], s.dl[rows, cols] = split(value)
        a, b = s.a32[rows, cols], s.b32[rows, cols]
        rest = a * (1 / 24) + b * (1 / 120) + value * (1 / 720)
        s.qh[rows, cols], s.ql[rows, cols] = split(rest)
        s.a32[rows, cols] = a + b * 0.5 + value * (1 / 6)

    mirrored(s.ah, s.al, s.bh, s.bl, -1, put)


def last_step(s, wh, wl):
    m = s.ah.shape[0]
    for cs in pieces(m, 256):
        value = dot3(s.dh, s.dl, s.qh, s.ql, cs) + s.a32[:, cs]
        for rs in pieces(m, 256):
            part = value[rs, :]
            if rs == cs:
                part = part + unit(part.shape)
            wh[rs, cs], wl[rs, cs] = split(part)


def unit(shape):
    return (
        lax.broadcasted_iota(jnp.int32, shape, 0) == lax.broadcasted_iota(jnp.int32, shape, 1)
    ).astype(f32)


def inside(x):
    return pltpu.with_memory_space_constraint(x, pltpu.VMEM)


def outside(x):
    return pltpu.with_memory_space_constraint(x, pltpu.HBM)


class Work:
    names = ("a32", "b32", "ah", "al", "bh", "bl", "dh", "dl", "qh", "ql")

    def __init__(self, refs):
        for name, ref in zip(self.names, refs):
            setattr(self, name, ref)

    @classmethod
    def shapes(cls, m):
        return [pltpu.VMEM((m, m), f32)] * 2 + [pltpu.VMEM((m, m), bf16)] * 8


def propagators(rows, picked, works, table, wh, wl, slots):
    count = rows.shape[1] // 2
    for row, s in zip(picked, works):
        amps = [rows[row, c] for c in range(count)]
        picks = [rows[row, count + c].astype(jnp.int32) for c in range(count)]
        generator(amps, picks, table, s)
    for s in works:
        square_step(s)
    for s in works:
        cube_step(s)
    for slot, s in zip(slots, works):
        last_step(s, wh.at[slot], wl.at[slot])


def load_kernel(controls, drift, table, sems):
    kinds = controls.shape[0]

    def copy(k):
        return pltpu.make_async_copy(controls.at[k], table.at[k], sems.at[k])

    last = pltpu.make_async_copy(drift, table.at[kinds], sems.at[kinds])
    copies = [copy(k) for k in range(kinds)] + [last]
    for each in copies:
        each.start()
    at = 0
    while at <= kinds:
        group = range(at, at + max((kinds + 1 - at) // 2, 1))
        at = group.stop
        for k in group:
            copies[k].wait()
        for k in group:
            skewed(table.at[k])


def works_of(scratch):
    size = len(Work.names)
    return [Work(scratch[at : at + size]) for at in range(0, len(scratch), size)]


def build_kernel(first, rows, table, *refs):
    size = len(Work.names)
    width = rows.shape[0]
    wh, wl = refs[-2 - width * size : -width * size]
    slots = [first + n for n in range(width)]
    propagators(rows, range(width), works_of(refs[-width * size :]), table, wh, wl, slots)


def multiply(ah, al, bh, bl):
    for cs in pieces(ah.shape[0], 256):
        yield cs, dot3(ah, al, bh, bl, cs)


def chain_kernel(
    place, rows, table, early_h, early_l, run, lh, ll, oh, ol,
    wh, wl, th, tl, qh, ql, bh, bl, *scratch
):
    half, m = early_h.shape[:2]
    fine = place[1]
    inner = fine & (half - 1)
    upper = jnp.where(fine < half, 1, 0)
    propagators(rows, range(half), works_of(scratch), table, wh, wl, range(half))
    for rs in pieces(m, 64):
        high, low = early_h[inner, rs, :], early_l[inner, rs, :]
        qh[0, rs, :], ql[0, rs, :] = high, low
        bh[0, rs, :], bl[0, rs, :] = high, low
    for step in range(1, half):
        slot = step ^ inner
        side = jnp.where(step <= inner, 0, 1)
        for cs, value in multiply(early_h.at[slot], early_l.at[slot], qh.at[0], ql.at[0]):
            high, low = split(value)
            qh[0, :, cs], ql[0, :, cs] = high, low
            bh[side, :, cs], bl[side, :, cs] = high, low
    for rs in pieces(m, 64):
        lh[rs, :], ll[rs, :] = bh[0, rs, :], bl[0, rs, :]
    level = [(wh.at[step ^ inner], wl.at[step ^ inner]) for step in range(half)]
    free = 0
    while len(level) > 1:
        above = []
        for n in range(0, len(level), 2):
            goal = (qh.at[1], ql.at[1]) if len(level) == 2 else (th.at[free], tl.at[free])
            free += 1
            for cs, value in multiply(*level[n + 1], *level[n]):
                goal[0][:, cs], goal[1][:, cs] = split(value)
            above.append(goal)
        level = above
    for cs, value in multiply(qh.at[upper], ql.at[upper], qh.at[1 - upper], ql.at[1 - upper]):
        run[:, cs] = value
    for rs in pieces(m, 64):
        oh[rs, :], ol[rs, :] = qh[1, rs, :], ql[1, rs, :]

    @pl.when((place[0] != 0) & (fine >= half))
    def _():
        for cs, value in multiply(bh.at[0], bl.at[0], qh.at[1], ql.at[1]):
            lh[:, cs], ll[:, cs] = split(value)


def long_kernel(order, place, rows, table, run, lh, ll, wh, wl, rh, rl, *scratch):
    works = works_of(scratch)
    m = run.shape[0]
    fine = place[1]
    for rs in pieces(m, 256):
        for cs in pieces(m, 256):
            shape = (rs.stop - rs.start, cs.stop - cs.start)
            rh[rs, cs], rl[rs, cs] = split(unit(shape) if rs == cs else jnp.zeros(shape, f32))

    def pair(n, carry):
        steps = [2 * n, 2 * n + 1]
        propagators(rows, [step ^ fine for step in steps], works, table, wh, wl, range(2))
        for k, step in enumerate(steps):
            for cs, value in multiply(wh.at[k], wl.at[k], rh, rl):
                run[:, cs] = value
                rh[:, cs], rl[:, cs] = split(value)

            @pl.when(step == fine)
            def _():
                for rs in pieces(m, 64):
                    lh[rs, :], ll[rs, :] = rh[rs, :], rl[rs, :]

        return carry

    lax.fori_loop(0, order // 2, pair, 0)


def multiply_nt(ah, al, bh, bl, rows=slice(None)):
    for cs in pieces(bh.shape[0], 256):
        yield cs, (
            dot_nt(ah[rows, :], bh[cs, :]) + dot_nt(ah[rows, :], bl[cs, :]) + dot_nt(al[rows, :], bh[cs, :])
        )


def turn_kernel(half, place, run, target, lh, ll, *refs):
    below = refs[: len(refs) - 10]
    eh, el, fh, fl, bh, bl, th, tl, ph, plo = refs[len(refs) - 10 :]
    m = run.shape[0]
    for rs in pieces(m, 32):
        bh[rs, :], bl[rs, :] = split(run[rs, :])
    later = (place[0] == 0) & (place[1] >= half) if below else False

    @pl.when(jnp.logical_not(later))
    def _():
        for rs in pieces(m, 64):
            ph[rs, :], plo[rs, :] = lh[rs, :], ll[rs, :]

    if below:

        @pl.when(later)
        def _():
            for cs, value in multiply(lh, ll, *below):
                ph[:, cs], plo[:, cs] = split(value)

    @pl.when(place[0] == 0)
    def _():
        for rs in pieces(m, 32):
            th[rs, :], tl[rs, :] = split(target[rs, :])
        for cs, value in multiply_nt(ph, plo, bh, bl):
            eh[:, cs], el[:, cs] = split(value)
        for cs, value in multiply_nt(ph, plo, th, tl):
            fh[:, cs], fl[:, cs] = split(value)

    @pl.when(place[0] != 0)
    def _():
        for ti in pieces(m, 128):
            for tj in pieces(m, 128):
                th[ti, tj], tl[ti, tj] = split(target[tj, ti].T)
        for cs, value in multiply(th, tl, bh, bl):
            eh[:, cs], el[:, cs] = split(value)
        for rs in pieces(m, 64):
            fh[rs, :], fl[rs, :] = ph[rs, :], plo[rs, :]


def final_kernel(place, picks, got, eh, el, fh, fl, table, out, gh, gl, x32, ph, plo, kh, kl, uh, ul):
    m = got.shape[0]
    count = picks.shape[1]

    def put(tiles_of):
        totals = [jnp.zeros((8, min(m, 128)), f32)] * count
        for ti, tj, tile in tiles_of:
            for c in range(count):
                part = table[picks[0, c], ti, tj] * tile
                for at in range(0, part.shape[0], 8):
                    totals[c] = totals[c] + part[at : at + 8, :]
        for c in range(count):
            out[0, c] = jnp.sum(totals[c])

    def receive():
        for rs in pieces(m, 32):
            gh[rs, :], gl[rs, :] = split(got[rs, :])

    @pl.when(place[0] == 0)
    def _():
        receive()
        for cs, value in multiply(fh, fl, gh, gl):
            kh[:, cs], kl[:, cs] = split(value)
        for cs, value in multiply_nt(eh, el, kh, kl):
            x32[:, cs] = value

        def tiles_of():
            for ti, tj in lower_tiles(m):
                yield ti, tj, x32[ti, tj] if ti == tj else x32[ti, tj] - x32[tj, ti].T

        put(tiles_of())

    @pl.when(place[0] != 0)
    def _():
        receive()
        for cs, value in multiply(eh, el, gh, gl):
            x32[:, cs] = value
        for cs, value in multiply(fh, fl, gh, gl):
            ph[:, cs], plo[:, cs] = split(value)
        for ti, tj in lower_tiles(m):
            value = 0.5 * (x32[tj, ti].T - x32[ti, tj])
            kh[ti, tj], kl[ti, tj] = split(value)
            if ti != tj:
                kh[tj, ti], kl[tj, ti] = split(-value.T)
        for cs, value in multiply(ph, plo, kh, kl):
            uh[:, cs], ul[:, cs] = split(value)

        def tiles_of():
            for rs in pieces(m, 256):
                for cs, value in multiply_nt(uh, ul, ph.at[: rs.stop], plo.at[: rs.stop], rs):
                    for ti, tj in lower_tiles(m):
                        if rs.start <= ti.start < rs.stop and cs.start <= tj.start < cs.stop:
                            tile = value[
                                ti.start - rs.start : ti.stop - rs.start, tj.start - cs.start : tj.stop - cs.start
                            ]
                            yield ti, tj, tile if ti == tj else tile + tile

        put(tiles_of())


def on_device(amplitudes, control_index, controls, drift_term, target):
    m = target.shape[0]
    kinds, count = controls.shape[0], amplitudes.shape[1]
    order = lax.axis_size("fine")
    assert amplitudes.shape[0] == 1 and lax.axis_size("coarse") == 2
    assert order & (order - 1) == 0 and order >= 4
    place = jnp.stack([lax.axis_index("coarse"), lax.axis_index("fine")]).astype(jnp.int32)
    square, half = pltpu.VMEM((m, m), f32), pltpu.VMEM((m, m), bf16)
    full = pltpu.VMEM((m, m), f32)
    short = order <= 8

    def params(mib):
        return pltpu.CompilerParams(vmem_limit_bytes=mib << 20)

    def cost(products):
        return pl.CostEstimate(
            flops=6 * products * m**3, bytes_accessed=12 * products * m * m, transcendentals=0
        )

    rows = fresh = coming = None
    early = ()
    bit = 1
    while bit < order:
        swap = [(i, i ^ bit) for i in range(order)]
        if bit == 1:
            pairs = (amplitudes, control_index), lax.ppermute((amplitudes, control_index), "fine", swap)
        else:
            coming = lax.ppermute(rows, "fine", swap)
        if bit == 1:
            table = pl.pallas_call(
                load_kernel,
                out_shape=pltpu.VMEM((kinds + 1, m, m), f32),
                in_specs=[HBM, HBM],
                out_specs=VMEM,
                scratch_shapes=[pltpu.SemaphoreType.DMA((kinds + 1,))],
                compiler_params=params(LOAD_MIB),
                cost_estimate=cost(2),
                name="load",
            )(outside(controls), outside(drift_term))
        elif short:
            width = fresh.shape[0]
            early = pl.pallas_call(
                functools.partial(build_kernel, bit - width),
                out_shape=(pltpu.VMEM((order // 2, m, m), bf16),) * 2,
                in_specs=[SMEM] + [VMEM] * (1 + len(early)),
                out_specs=(VMEM, VMEM),
                scratch_shapes=Work.shapes(m) * width,
                input_output_aliases={2: 0, 3: 1} if early else {},
                compiler_params=params(BUILD_MIB),
                cost_estimate=cost(4 * width),
                name="build",
            )(fresh, inside(table), *map(inside, early))
        if bit == 1:
            amps, picks = lax.optimization_barrier([jnp.concatenate(each, axis=0) for each in zip(*pairs)])
            rows = fresh = jnp.concatenate([amps, picks.astype(f32)], axis=1)
        else:
            rows, fresh = jnp.concatenate([rows, coming], axis=0), coming
        bit *= 2

    if short:
        kernel, taken = chain_kernel, (table, *early)
        outs = (square,) + (half,) * 4
        halves = [pltpu.VMEM((order // 2, m, m), bf16)] * 2
        scratch = halves * 2 + [pltpu.VMEM((2, m, m), bf16)] * 4 + Work.shapes(m) * (order // 2)
    else:
        kernel, taken, fresh = functools.partial(long_kernel, order), (table,), rows
        outs = (square, half, half)
        scratch = [pltpu.VMEM((2, m, m), bf16)] * 2 + [half] * 2 + Work.shapes(m) * 2
    run, *products = pl.pallas_call(
        kernel,
        out_shape=outs,
        in_specs=[SMEM] * 2 + [VMEM] * len(taken),
        out_specs=(VMEM,) * len(outs),
        scratch_shapes=scratch,
        compiler_params=params(CHAIN_MIB),
        cost_estimate=cost(23),
        name="chain",
    )(place, fresh, *map(inside, taken))
    got = lax.ppermute(run, "coarse", [(0, 1), (1, 0)])
    turned = pl.pallas_call(
        functools.partial(turn_kernel, order // 2),
        out_shape=(half,) * 4,
        in_specs=[SMEM] + [VMEM] * (2 + len(products)),
        out_specs=(VMEM,) * 4,
        scratch_shapes=[half] * 6,
        compiler_params=params(TURN_MIB),
        cost_estimate=cost(2),
        name="turn",
    )(place, inside(run), target, *map(inside, products))
    return pl.pallas_call(
        final_kernel,
        out_shape=jax.ShapeDtypeStruct((1, count), f32),
        in_specs=[SMEM, SMEM] + [VMEM] * 6,
        out_specs=SMEM,
        scratch_shapes=[half] * 2 + [full] + [half] * 6,
        compiler_params=params(FINAL_MIB),
        name="final",
    )(place, control_index, got, *map(inside, (*turned, table)))


LOAD_MIB = 4
BUILD_MIB = 14
CHAIN_MIB = 36
TURN_MIB = 6
FINAL_MIB = 12


def solution(mesh):
    placed = (
        P(("groups", "coarse", "fine"), None),
        P(("groups", "coarse", "fine"), None),
        P(),
        P(),
        P("groups", None),
    )
    return jax.shard_map(
        on_device,
        mesh=mesh,
        in_specs=placed,
        out_specs=P(("groups", "coarse", "fine"), None),
        check_vma=False,
    )
```
